256 devices in a mesh: seq: 32 (over z, x), tp: 8 (over y, core).
Axes of the slice: x: 4, y: 4, z: 8, core: 2. Of those that a mesh axis runs over, the one named last changes fastest.
Arguments:
- grad_out: bfloat16 [8192, 4096], P('seq', 'tp'), may hold values from -6 to 6
- out_weight: bfloat16 [4096, 4096], P('tp'), may hold values from -0.09375 to 0.09375
- queries: bfloat16 [8192, 4096], P('seq', 'tp'), may hold values from -45 to 45
- keys: bfloat16 [8192, 4096], P('seq', 'tp'), may hold values from -4 to 4
- values: bfloat16 [8192, 4096], P('seq', 'tp'), may hold values from -6 to 6
- visible: int32 [64, 3], replicated, may hold values from 0 to 63, as said below
- live: int32 [64], replicated, may hold values from 1 to 3
Outputs:
- grad_queries: bfloat16 [8192, 4096], P('seq', 'tp')
- grad_keys: bfloat16 [8192, 4096], P('seq', 'tp')
- grad_values: bfloat16 [8192, 4096], P('seq', 'tp')
The draws below stay inside these ranges and needn't reach their ends.
Inputs may be any that keep to these rules, and one draw needn't show every extreme that they name: `visible`: row a lists blocks that lie on other shards than a's (block b lies on shard b // 2); the rows of one shard never list a block twice, and list at most 1 block of any one other shard, a bound that some shard reaches.
All inputs are finite; a program needn't handle non-finite values.
Results may differ from the reference program's by a relative error of at most 0.014.
Values may be sent and summed in bfloat16 or wider, within the bound.
A program may use at most 128 MiB of HBM per device.

```python
import math
import jax
import jax.numpy as jnp
from jax import lax

D = 4096
HEADS = 32
D_HEAD = 128
BLK = 128
BLK_DEV = 2
NREM = 3
NBLK = 64
TOKENS = 8192


def paired_rows(key, part):
    array_shape = (TOKENS, HEADS * D_HEAD)
    keys_drawn = jnp.clip(jax.random.normal(jax.random.fold_in(key, 71), array_shape, jnp.float32), -4.0, 4.0)
    queries_drawn = jnp.clip(jax.random.normal(jax.random.fold_in(key, 72), array_shape, jnp.float32), -4.0, 4.0)
    return (queries_drawn, keys_drawn)


def draw_queries(key, part):
    return paired_rows(key, part)[0].astype(jnp.bfloat16)


def draw_keys(key, part):
    return paired_rows(key, part)[1].astype(jnp.bfloat16)


def draw_visible(key, part):
    shard_count = NBLK // BLK_DEV
    others = shard_count - 1
    entries = BLK_DEV * NREM

    def one_shard(shard):
        shard_key = jax.random.fold_in(key, shard)
        ordering = jax.random.permutation(jax.random.fold_in(shard_key, 81), others)
        offsets = jax.random.randint(jax.random.fold_in(shard_key, 82), (shard_count,), 0, BLK_DEV)
        entry = jnp.arange(entries)
        owner = (shard + 1 + ordering[entry % others]) % shard_count
        within = (offsets[owner] + entry // others) % BLK_DEV
        return owner * BLK_DEV + within
    listed = jax.vmap(one_shard)(jnp.arange(shard_count))
    return listed.reshape(NBLK, NREM).astype(jnp.int32)


def draw_live(key, part):
    drawn = jax.random.randint(jax.random.fold_in(key, 91), (NBLK,), 1, NREM + 1)
    return jnp.where(jnp.arange(NBLK) < BLK_DEV, NREM, drawn).astype(jnp.int32)


def block_levels(key, shape, split, smallest, largest):
    def one(dim, blocks):
        draws = jax.random.uniform(jax.random.fold_in(jax.random.fold_in(key, 6), dim), (blocks,), jnp.float32, smallest / len(split), largest / len(split))
        return jnp.repeat(jnp.exp(draws), shape[dim] // blocks).reshape((-1,) + (1,) * (len(shape) - dim - 1))

    loudness = one(*split[0])
    for cut in split[1:]:
        loudness = loudness * one(*cut)
    return loudness


def gaussian(key, dims, width, reach, pieces=(), kind=jnp.bfloat16):
    loudness = block_levels(key, dims, pieces, -0.22, 0.18) if pieces else 1.0
    array = jax.random.normal(key, dims, jnp.float32) * width * loudness
    return jnp.minimum(jnp.maximum(array, -reach), reach).astype(kind)


def setup_inputs(seed: int = 0) -> dict:
    seeds = jax.random.split(jax.random.key(seed), 8)
    return {
        "grad_out": gaussian(seeds[0], (TOKENS, D), 1.0, 6.0, ((0, 32), (1, 8))),
        "out_weight": gaussian(seeds[1], (HEADS * D_HEAD, D), D ** -0.5, 0.09375, ((0, 8),)),
        "queries": draw_queries(jax.random.fold_in(seeds[7], 71), 0),
        "keys": draw_keys(jax.random.fold_in(seeds[7], 71), 0),
        "values": gaussian(seeds[4], (TOKENS, HEADS * D_HEAD), 1.0, 6.0, ((0, 32), (1, 8))),
        "visible": draw_visible(jax.random.fold_in(seeds[7], 71), 0),
        "live": draw_live(jax.random.fold_in(seeds[7], 71), 0),
    }


def rounded(array_in):
    return lax.optimization_barrier(array_in.astype(jnp.bfloat16)).astype(jnp.float32)

def reference(grad_out, out_weight, queries, keys, values, visible, live):
    head_count = HEADS
    feature_width = HEADS * D_HEAD
    row_count = BLK_DEV * BLK
    shard_count = NBLK // BLK_DEV
    scaling = 1.0 / math.sqrt(D_HEAD)
    key_blocks = keys.reshape(NBLK, BLK, feature_width)
    value_blocks = values.reshape(NBLK, BLK, feature_width)

    def one_shard(carry, shard):
        grad_key_acc, grad_value_acc = carry
        first_row = (shard * row_count).astype(jnp.int32)
        first_block = (shard * BLK_DEV).astype(jnp.int32)
        upstream = lax.dynamic_slice_in_dim(grad_out, first_row, row_count, 0)
        dout = jnp.dot(upstream, out_weight.T, preferred_element_type=jnp.float32).astype(jnp.bfloat16)
        dout_rows = dout.astype(jnp.float32).reshape(BLK_DEV, BLK, head_count, D_HEAD)
        query_rows = lax.dynamic_slice_in_dim(queries, first_row, row_count, 0).astype(jnp.float32).reshape(BLK_DEV, BLK, head_count, D_HEAD)
        key_near = lax.dynamic_slice_in_dim(keys, first_row, row_count, 0).astype(jnp.float32).reshape(row_count, head_count, D_HEAD)
        value_near = lax.dynamic_slice_in_dim(values, first_row, row_count, 0).astype(jnp.float32).reshape(row_count, head_count, D_HEAD)
        listed = lax.dynamic_slice_in_dim(visible, first_block, BLK_DEV, 0).reshape(BLK_DEV * NREM).astype(jnp.int32)
        counts = lax.dynamic_slice_in_dim(live, first_block, BLK_DEV, 0)
        key_far = jnp.take(key_blocks, listed, axis=0).astype(jnp.float32).reshape(BLK_DEV, NREM * BLK, head_count, D_HEAD)
        value_far = jnp.take(value_blocks, listed, axis=0).astype(jnp.float32).reshape(BLK_DEV, NREM * BLK, head_count, D_HEAD)
        seen_mask = jnp.repeat(jnp.arange(NREM, dtype=jnp.int32)[None, :] < counts[:, None], BLK, axis=1)
        near_scores = jnp.einsum('aihd,jhd->ahij', query_rows, key_near) * scaling
        far_scores = jnp.einsum('aihd,ajhd->ahij', query_rows, key_far) * scaling
        far_scores = jnp.where(seen_mask[:, None, None, :], far_scores, -1e+30)
        highest = jnp.maximum(lax.optimization_barrier(jnp.max(near_scores, axis=3)), lax.optimization_barrier(jnp.max(far_scores, axis=3)))[..., None]
        near_exp = jnp.exp(near_scores - highest)
        far_exp = jnp.exp(far_scores - highest)
        totals = lax.optimization_barrier(jnp.sum(near_exp, axis=3, keepdims=True)) + lax.optimization_barrier(jnp.sum(far_exp, axis=3, keepdims=True))
        near_probs = near_exp / totals
        far_probs = far_exp / totals
        near_grad = jnp.einsum('aihd,jhd->ahij', dout_rows, value_near)
        far_grad = jnp.einsum('aihd,ajhd->ahij', dout_rows, value_far)
        row_delta = lax.optimization_barrier(jnp.sum(near_probs * near_grad, axis=3, keepdims=True)) + lax.optimization_barrier(jnp.sum(far_probs * far_grad, axis=3, keepdims=True))
        near_ds = rounded(near_probs * (near_grad - row_delta) * scaling)
        far_ds = rounded(far_probs * (far_grad - row_delta) * scaling)
        grad_query = jnp.einsum('ahij,jhd->aihd', near_ds, key_near) + jnp.einsum('ahij,ajhd->aihd', far_ds, key_far)
        grad_query = grad_query.reshape(row_count, feature_width).astype(jnp.bfloat16)
        near_key_term = jnp.einsum('ahij,aihd->jhd', near_ds, query_rows).reshape(BLK_DEV, BLK, feature_width)
        near_value_term = jnp.einsum('ahij,aihd->jhd', rounded(near_probs), dout_rows).reshape(BLK_DEV, BLK, feature_width)
        far_key_term = rounded(jnp.einsum('ahij,aihd->ajhd', far_ds, query_rows)).reshape(BLK_DEV * NREM, BLK, feature_width)
        far_value_term = rounded(jnp.einsum('ahij,aihd->ajhd', rounded(far_probs), dout_rows)).reshape(BLK_DEV * NREM, BLK, feature_width)
        grad_key_acc = grad_key_acc.at[listed].add(far_key_term)
        grad_value_acc = grad_value_acc.at[listed].add(far_value_term)
        own_keys = lax.dynamic_slice_in_dim(grad_key_acc, first_block, BLK_DEV, 0) + near_key_term
        own_values = lax.dynamic_slice_in_dim(grad_value_acc, first_block, BLK_DEV, 0) + near_value_term
        grad_key_acc = lax.dynamic_update_slice_in_dim(grad_key_acc, own_keys, first_block, 0)
        grad_value_acc = lax.dynamic_update_slice_in_dim(grad_value_acc, own_values, first_block, 0)
        return ((grad_key_acc, grad_value_acc), grad_query)
    start = (jnp.zeros((NBLK, BLK, feature_width), jnp.float32), jnp.zeros((NBLK, BLK, feature_width), jnp.float32))
    (grad_key_acc, grad_value_acc), grad_query_all = lax.scan(one_shard, start, jnp.arange(shard_count, dtype=jnp.int32))
    grad_queries = grad_query_all.reshape(TOKENS, feature_width)
    grad_keys = grad_key_acc.reshape(TOKENS, feature_width).astype(jnp.bfloat16)
    grad_values = grad_value_acc.reshape(TOKENS, feature_width).astype(jnp.bfloat16)
    return (grad_queries, grad_keys, grad_values)
```

```python
import functools
import math

import jax
import jax.numpy as jnp
from jax import lax
from jax.experimental import pallas as pl
from jax.experimental.pallas import tpu as pltpu
from jax.sharding import PartitionSpec as P

MESH = pl.DeviceIdType.MESH
BF16 = jnp.bfloat16
F32 = jnp.float32

D_HEAD = 128
BLK = 128
BLK_DEV = 2
NREM = 3
ENTRIES = BLK_DEV * NREM
NZ, NX = 8, 4
SHARDS = NZ * NX
NBLK = SHARDS * BLK_DEV
CHUNK = 32
HALF = CHUNK // 2
SCALE = 1.0 / math.sqrt(D_HEAD)

SERVED = (
    [(dz, dx, 0, CHUNK) for dz in (0, 1, NZ - 1) for dx in range(NX)]
    + [(2, dx, HALF, HALF) for dx in range(NX)]
    + [(NZ - 2, dx, 0, HALF) for dx in range(NX)]
)
SLOT = {(dz, dx): i for i, (dz, dx, _, _) in enumerate(SERVED)}
FULL_SLOTS = 16

P1K, P1V, P2K, P2V, R1V, R1K, R2V, R2K, GATHER = range(9)


def dot(a, b, contract):
    return lax.dot_general(a, b, ((contract[:1], contract[1:]), ((), ())), preferred_element_type=F32)


def kernel(
    tp_size,
    visible, live, inverse,
    g_hbm, w_hbm, q_hbm, k_hbm, v_hbm,
    dq_ref, dk_ref, dv_ref,
    g_v, w_v, q_v, k_v, v_v, g_all, do_v,
    hold_k, hold_v, pick_k, pick_v, far_k, far_v,
    back_v, back_k, got_v, got_k, sum_v, sum_k, fin_v, fin_k,
    near_p, far_p, near_dv, near_dk,
    send, recv, load,
):
    me = lax.axis_index("seq")
    tp = lax.axis_index("tp")
    z, x = lax.div(me, NX), lax.rem(me, NX)
    others = [(dz, dx) for dz in range(NZ) for dx in range(NX) if (dz, dx) != (0, 0)]

    def shard_at(dz, dx):
        return lax.rem(z + dz, NZ) * NX + lax.rem(x + dx, NX)

    barrier = pltpu.get_barrier_semaphore()
    for dz, dx in others:
        pl.semaphore_signal(barrier, inc=1, device_id=(shard_at(dz, dx), tp), device_id_type=MESH)
    for dt in range(1, tp_size):
        pl.semaphore_signal(barrier, inc=1, device_id=(me, lax.rem(tp + dt, tp_size)), device_id_type=MESH)
    loads = [
        pltpu.make_async_copy(src, dst, load.at[i])
        for i, (src, dst) in enumerate(((k_hbm, k_v), (g_hbm, g_v), (v_hbm, v_v), (q_hbm, q_v), (w_hbm, w_v)))
    ]
    for copy in loads:
        copy.start()
    loads[0].wait()
    loads[1].wait()
    loads[2].wait()
    pl.semaphore_wait(barrier, len(others) + tp_size - 1)

    def remote(src, dst, phase, device):
        pltpu.make_async_remote_copy(
            src_ref=src, dst_ref=dst, send_sem=send.at[phase], recv_sem=recv.at[phase],
            device_id=device, device_id_type=MESH,
        ).start()

    def local(src, dst, phase):
        pltpu.make_async_copy(src, dst, recv.at[phase]).start()

    def arrived(ref, phase):
        pltpu.make_async_copy(ref, ref, recv.at[phase]).wait()

    def sent(ref, phase):
        pltpu.make_async_copy(ref, ref, send.at[phase]).wait()

    def chunk_of(zz):
        return pl.multiple_of(lax.rem(zz, NX) * CHUNK, CHUNK)

    def lanes_of(head):
        return pl.ds(pl.multiple_of(head * D_HEAD, D_HEAD), D_HEAD)

    my_blocks = pl.ds(me * BLK_DEV, BLK_DEV)

    def spread(own, hold, phase):
        def part(dz, dx):
            return own.at[:, pl.ds(chunk_of(z + dz), CHUNK), lanes_of(lax.rem(x + dx, NX))]

        for dz, dx in others:
            remote(part(dz, dx), hold.at[my_blocks], phase, (shard_at(dz, dx), tp))
        local(part(0, 0), hold.at[my_blocks], phase)

    spread(k_v, hold_k, P1K)
    for dt in range(1, tp_size):
        remote(g_v, g_all.at[tp], GATHER, (me, lax.rem(tp + dt, tp_size)))
    local(g_v, g_all.at[tp], GATHER)
    spread(v_v, hold_v, P1V)

    loads[3].wait()

    def near_scores(head, _):
        lanes = lanes_of(head)
        keys = k_v[:, :, lanes].reshape(BLK_DEV * BLK, D_HEAD)
        near_p[head] = dot(keys, q_v[:, lanes], (1, 1)) * SCALE
        return 0

    lax.fori_loop(0, NX, near_scores, 0)

    def forward(hold, pick, far, phase):
        for i, (dz, dx, first, rows) in enumerate(SERVED):
            shard = shard_at(dz, dx)
            for e in range(ENTRIES):
                block = visible[shard * ENTRIES + e]
                pick[i, e, first : first + rows] = hold[block, first : first + rows]
        for i, (dz, dx, first, rows) in enumerate(SERVED):
            src = pick.at[i, :, pl.ds(first, rows)]
            dst = far.at[:, x, pl.ds(pl.multiple_of(chunk_of(z) + first, HALF), rows)]
            if i == 0:
                local(src, dst, phase)
            else:
                remote(src, dst, phase, (shard_at(dz, dx), tp))

    arrived(hold_k, P1K)
    forward(hold_k, pick_k, far_k, P2K)
    arrived(hold_v, P1V)
    forward(hold_v, pick_v, far_v, P2V)

    loads[4].wait()
    arrived(g_all, GATHER)
    width = g_v.shape[1]
    total = dot(g_all[0], w_v[:, :width], (1, 1))
    for t in range(1, tp_size):
        total += dot(g_all[t], w_v[:, t * width : (t + 1) * width], (1, 1))
    do_v[...] = total.astype(BF16)

    def return_far(back, got, phase, dx):
        head = lax.rem(x + dx, NX)
        for dz in (0, 1, NZ - 1, 2, NZ - 2):
            slot = SLOT[((NZ - dz) % NZ, (NX - dx) % NX)]
            _, _, first, rows = SERVED[slot]
            src = back.at[:, head, pl.ds(pl.multiple_of(chunk_of(z + dz) + first, HALF), rows)]
            dst = got.at[slot, pl.ds(0, ENTRIES), pl.ds(first, rows)]
            if slot == 0:
                local(src, dst, phase)
            else:
                remote(src, dst, phase, (shard_at(dz, dx), tp))

    arrived(far_k, P2K)
    for dx in range(NX):
        head = lax.rem(x + dx, NX)
        lanes = lanes_of(head)
        pieces = []
        for a in range(BLK_DEV):
            rows = slice(a * BLK, (a + 1) * BLK)
            near = near_p[head, :, rows]
            keys = far_k[a * NREM : (a + 1) * NREM, head].reshape(NREM * BLK, D_HEAD)
            far = dot(keys, q_v[rows, lanes], (1, 1)) * SCALE
            count = live[me * BLK_DEV + a]
            entry = lax.broadcasted_iota(jnp.int32, far.shape, 0) // BLK
            far = jnp.where(entry < count, far, -1e30)
            highest = jnp.maximum(jnp.max(near, axis=0, keepdims=True), jnp.max(far, axis=0, keepdims=True))
            near = jnp.exp(near - highest)
            far = jnp.exp(far - highest)
            scale = 1.0 / (jnp.sum(near, axis=0, keepdims=True) + jnp.sum(far, axis=0, keepdims=True))
            near = near * scale
            far = far * scale
            near_p[head, :, rows] = near
            far_p[head, a] = far
            far_dv = dot(far.astype(BF16), do_v[rows, lanes], (1, 0)).astype(BF16)
            back_v[a * NREM : (a + 1) * NREM, head] = far_dv.reshape(NREM, BLK, D_HEAD)
            pieces.append(near.astype(BF16))
        return_far(back_v, got_v, R1V, dx)
        near_dv[head] = dot(jnp.concatenate(pieces, axis=1), do_v[:, lanes], (1, 0))

    arrived(far_v, P2V)
    for dx in range(NX):
        head = lax.rem(x + dx, NX)
        lanes = lanes_of(head)
        values = v_v[:, :, lanes].reshape(BLK_DEV * BLK, D_HEAD)
        near_grad = dot(values, do_v[:, lanes], (1, 1))
        pieces, fars = [], []
        for a in range(BLK_DEV):
            rows = slice(a * BLK, (a + 1) * BLK)
            far_values = far_v[a * NREM : (a + 1) * NREM, head].reshape(NREM * BLK, D_HEAD)
            grad = dot(far_values, do_v[rows, lanes], (1, 1))
            near, far = near_p[head, :, rows], far_p[head, a]
            own = near_grad[:, rows]
            delta = jnp.sum(near * own, axis=0, keepdims=True) + jnp.sum(far * grad, axis=0, keepdims=True)
            near = (near * (own - delta) * SCALE).astype(BF16)
            far = (far * (grad - delta) * SCALE).astype(BF16)
            far_dk = dot(far, q_v[rows, lanes], (1, 0)).astype(BF16)
            back_k[a * NREM : (a + 1) * NREM, head] = far_dk.reshape(NREM, BLK, D_HEAD)
            pieces.append(near)
            fars.append(far)
        return_far(back_k, got_k, R1K, dx)
        near = jnp.concatenate(pieces, axis=1)
        near_dk[head] = dot(near, q_v[:, lanes], (1, 0))
        keys = k_v[:, :, lanes].reshape(BLK_DEV * BLK, D_HEAD)
        near_dq = dot(near, keys, (0, 0))
        for a in range(BLK_DEV):
            rows = slice(a * BLK, (a + 1) * BLK)
            keys = far_k[a * NREM : (a + 1) * NREM, head].reshape(NREM * BLK, D_HEAD)
            dq_ref[rows, lanes] = (near_dq[rows] + dot(fars[a], keys, (0, 0))).astype(BF16)

    served = [shard_at(dz, dx) * NBLK for dz, dx, _, _ in SERVED]
    zeros = jnp.zeros((CHUNK, D_HEAD), BF16)

    def collect(got, sums, fin, phase):
        def one_block(block, _):
            upper = jnp.zeros((HALF, D_HEAD), F32)
            lower = jnp.zeros((HALF, D_HEAD), F32)
            for i, (_, _, first, rows) in enumerate(SERVED):
                e = inverse[served[i] + block]
                if first == 0:
                    upper += got[i, e, :HALF].astype(F32)
                if first + rows == CHUNK:
                    lower += got[i, e, HALF:].astype(F32)
            sums[block, :HALF] = upper.astype(BF16)
            sums[block, HALF:] = lower.astype(BF16)
            return 0

        lax.fori_loop(0, NBLK, one_block, 0)
        dst = fin.at[lax.div(z, NX), x, :, pl.ds(chunk_of(z), CHUNK)]
        for dz, dx in others:
            shard = shard_at(dz, dx)
            remote(sums.at[pl.ds(shard * BLK_DEV, BLK_DEV)], dst, phase, (shard, tp))
        local(sums.at[my_blocks], dst, phase)

    counted = (pl.ds(0, FULL_SLOTS), pl.ds(0, ENTRIES))
    for i in range(len(SERVED)):
        got_v[i, ENTRIES] = zeros
        got_k[i, ENTRIES] = zeros
    arrived(got_v.at[counted], R1V)
    collect(got_v, sum_v, fin_v, R2V)
    arrived(got_k.at[counted], R1K)
    collect(got_k, sum_k, fin_k, R2K)

    def finish(near, fin, out):
        for head in range(NX):
            total = near[head]
            for copy in range(2):
                total += fin[copy, head].reshape(BLK_DEV * BLK, D_HEAD).astype(F32)
            out[:, head * D_HEAD : (head + 1) * D_HEAD] = total.astype(BF16)

    arrived(fin_v, R2V)
    finish(near_dv, fin_v, dv_ref)
    arrived(fin_k, R2K)
    finish(near_dk, fin_k, dk_ref)

    most = pl.ds(0, NBLK - BLK_DEV)
    sent(hold_k.at[most], P1K)
    sent(hold_v.at[most], P1V)
    sent(g_all.at[pl.ds(0, tp_size - 1)], GATHER)
    fewer = (pl.ds(0, FULL_SLOTS - 1), pl.ds(0, ENTRIES))
    sent(pick_k.at[fewer], P2K)
    sent(pick_v.at[fewer], P2V)
    sent(got_v.at[fewer], R1V)
    sent(got_k.at[fewer], R1K)
    sent(sum_v.at[most], R2V)
    sent(sum_k.at[most], R2K)


def shards(tp_size, grad_out, out_weight, queries, keys, values, visible, live):
    rows, features = queries.shape
    heads = features // D_HEAD
    listed = visible.reshape(SHARDS, ENTRIES).astype(jnp.int32)
    blocks = jnp.arange(NBLK, dtype=jnp.int32)
    entry = jnp.arange(ENTRIES, dtype=jnp.int32)
    hit = listed[:, :, None] == blocks[None, None, :]
    inverse = jnp.min(jnp.where(hit, entry[None, :, None], ENTRIES), axis=1).reshape(-1)
    smem = pl.BlockSpec(memory_space=pltpu.SMEM)
    anywhere = pl.BlockSpec(memory_space=pl.ANY)
    vmem = pl.BlockSpec(memory_space=pltpu.VMEM)
    out = jax.ShapeDtypeStruct((rows, features), BF16)
    tiles = pltpu.VMEM((NBLK, CHUNK, D_HEAD), BF16)
    picked = pltpu.VMEM((len(SERVED), ENTRIES, CHUNK, D_HEAD), BF16)
    far = pltpu.VMEM((ENTRIES, heads, BLK, D_HEAD), BF16)
    got = pltpu.VMEM((len(SERVED), ENTRIES + 1, CHUNK, D_HEAD), BF16)
    fin = pltpu.VMEM((2, heads, BLK_DEV, BLK, D_HEAD), BF16)
    near = pltpu.VMEM((heads, rows, D_HEAD), F32)
    split = (BLK_DEV, BLK, features)
    return pl.pallas_call(
        functools.partial(kernel, tp_size),
        out_shape=(out, out, out),
        in_specs=[smem, smem, smem] + [anywhere] * 5,
        out_specs=(vmem, vmem, vmem),
        scratch_shapes=[
            pltpu.VMEM(grad_out.shape, BF16),
            pltpu.VMEM(out_weight.shape, BF16),
            pltpu.VMEM(queries.shape, BF16),
            pltpu.VMEM(split, BF16),
            pltpu.VMEM(split, BF16),
            pltpu.VMEM((tp_size,) + grad_out.shape, BF16),
            pltpu.VMEM(queries.shape, BF16),
            tiles, tiles, picked, picked, far, far,
            far, far, got, got, tiles, tiles, fin, fin,
            pltpu.VMEM((heads, rows, rows), F32),
            pltpu.VMEM((heads, BLK_DEV, NREM * BLK, BLK), F32),
            near, near,
            pltpu.SemaphoreType.DMA((9,)),
            pltpu.SemaphoreType.DMA((9,)),
            pltpu.SemaphoreType.DMA((5,)),
        ],
        compiler_params=pltpu.CompilerParams(
            collective_id=0, has_side_effects=True, vmem_limit_bytes=56 * 2**20
        ),
    )(
        listed.reshape(-1), live, inverse,
        grad_out, out_weight, queries, keys.reshape(split), values.reshape(split),
    )


def solution(mesh):
    placed = (
        P("seq", "tp"),
        P("tp", None),
        P("seq", "tp"),
        P("seq", "tp"),
        P("seq", "tp"),
        P(),
        P(),
    )
    return jax.shard_map(
        functools.partial(shards, mesh.shape["tp"]),
        mesh=mesh,
        in_specs=placed,
        out_specs=(P("seq", "tp"), P("seq", "tp"), P("seq", "tp")),
        check_vma=False,
    )
```

```python
import functools
import math

import jax
import jax.numpy as jnp
from jax import lax
from jax.experimental import pallas as pl
from jax.experimental.pallas import tpu as pltpu
from jax.sharding import PartitionSpec as P

MESH = pl.DeviceIdType.MESH
BF16 = jnp.bfloat16
F32 = jnp.float32

D_HEAD = 128
BLK = 128
BLK_DEV = 2
NREM = 3
ENTRIES = BLK_DEV * NREM
NZ, NX = 8, 4
SHARDS = NZ * NX
NBLK = SHARDS * BLK_DEV
CHUNK = 32
HALF = CHUNK // 2
SCALE = 1.0 / math.sqrt(D_HEAD)

SERVED = (
    [(dz, dx, 0, CHUNK) for dz in (0, 1, NZ - 1) for dx in range(NX)]
    + [(2, dx, HALF, HALF) for dx in range(NX)]
    + [(NZ - 2, dx, 0, HALF) for dx in range(NX)]
)
SLOT = {(dz, dx): i for i, (dz, dx, _, _) in enumerate(SERVED)}
FULL_SLOTS = 16

P1K, P1V, P2K, P2V, R1V, R1K, R2V, R2K, GATHER = range(9)


def dot(a, b, contract):
    return lax.dot_general(a, b, ((contract[:1], contract[1:]), ((), ())), preferred_element_type=F32)


def kernel(
    tp_size,
    visible, live, listed,
    g_hbm, w_hbm, q_hbm, k_hbm, v_hbm,
    dq_ref, dk_ref, dv_ref,
    g_v, w_v, q_v, k_v, v_v, g_all, do_v,
    hold_k, hold_v, pick_k, pick_v, far_k, far_v,
    back_v, back_k, got_v, got_k, sum_v, sum_k, fin_v, fin_k,
    near_p, far_p, near_dv, near_dk, found, inverse,
    send, recv, load,
):
    me = lax.axis_index("seq")
    tp = lax.axis_index("tp")
    z, x = lax.div(me, NX), lax.rem(me, NX)
    others = [(dz, dx) for dz in range(NZ) for dx in range(NX) if (dz, dx) != (0, 0)]

    def shard_at(dz, dx):
        return lax.rem(z + dz, NZ) * NX + lax.rem(x + dx, NX)

    barrier = pltpu.get_barrier_semaphore()
    for dz, dx in others:
        pl.semaphore_signal(barrier, inc=1, device_id=(shard_at(dz, dx), tp), device_id_type=MESH)
    for dt in range(1, tp_size):
        pl.semaphore_signal(barrier, inc=1, device_id=(me, lax.rem(tp + dt, tp_size)), device_id_type=MESH)
    loads = [
        pltpu.make_async_copy(src, dst, load.at[i])
        for i, (src, dst) in enumerate(((k_hbm, k_v), (g_hbm, g_v), (v_hbm, v_v), (q_hbm, q_v), (w_hbm, w_v)))
    ]
    for copy in loads:
        copy.start()
    shape = (NBLK, NBLK)
    block = lax.broadcasted_iota(jnp.int32, shape, 0)
    first_entry = lax.broadcasted_iota(jnp.int32, shape, 1) % BLK_DEV * NREM
    place = jnp.full(shape, ENTRIES, jnp.int32)
    for j in range(NREM):
        place = jnp.where(listed[j : j + 1, :] == block, first_entry + j, place)
    found[...] = place
    table = pltpu.make_async_copy(found, inverse, load.at[5])
    table.start()
    loads[0].wait()
    loads[1].wait()
    loads[2].wait()
    pl.semaphore_wait(barrier, len(others) + tp_size - 1)

    def remote(src, dst, phase, device):
        pltpu.make_async_remote_copy(
            src_ref=src, dst_ref=dst, send_sem=send.at[phase], recv_sem=recv.at[phase],
            device_id=device, device_id_type=MESH,
        ).start()

    def local(src, dst, phase):
        pltpu.make_async_copy(src, dst, recv.at[phase]).start()

    def arrived(ref, phase):
        pltpu.make_async_copy(ref, ref, recv.at[phase]).wait()

    def sent(ref, phase):
        pltpu.make_async_copy(ref, ref, send.at[phase]).wait()

    def chunk_of(zz):
        return pl.multiple_of(lax.rem(zz, NX) * CHUNK, CHUNK)

    def lanes_of(head):
        return pl.ds(pl.multiple_of(head * D_HEAD, D_HEAD), D_HEAD)

    my_blocks = pl.ds(me * BLK_DEV, BLK_DEV)

    def spread(own, hold, phase):
        def part(dz, dx):
            return own.at[:, pl.ds(chunk_of(z + dz), CHUNK), lanes_of(lax.rem(x + dx, NX))]

        for dz, dx in others:
            remote(part(dz, dx), hold.at[my_blocks], phase, (shard_at(dz, dx), tp))
        local(part(0, 0), hold.at[my_blocks], phase)

    spread(k_v, hold_k, P1K)
    for dt in range(1, tp_size):
        remote(g_v, g_all.at[tp], GATHER, (me, lax.rem(tp + dt, tp_size)))
    local(g_v, g_all.at[tp], GATHER)
    spread(v_v, hold_v, P1V)

    loads[3].wait()

    def near_scores(head, _):
        lanes = lanes_of(head)
        keys = k_v[:, :, lanes].reshape(BLK_DEV * BLK, D_HEAD)
        near_p[head] = dot(keys, q_v[:, lanes], (1, 1)) * SCALE
        return 0

    lax.fori_loop(0, NX, near_scores, 0)

    def forward(hold, pick, far, phase):
        for i, (dz, dx, first, rows) in enumerate(SERVED):
            shard = shard_at(dz, dx)
            for e in range(ENTRIES):
                block = visible[e % NREM, shard * BLK_DEV + e // NREM]
                pick[i, e, first : first + rows] = hold[block, first : first + rows]
        for i, (dz, dx, first, rows) in enumerate(SERVED):
            src = pick.at[i, :, pl.ds(first, rows)]
            dst = far.at[:, x, pl.ds(pl.multiple_of(chunk_of(z) + first, HALF), rows)]
            if i == 0:
                local(src, dst, phase)
            else:
                remote(src, dst, phase, (shard_at(dz, dx), tp))

    arrived(hold_k, P1K)
    forward(hold_k, pick_k, far_k, P2K)
    arrived(hold_v, P1V)
    forward(hold_v, pick_v, far_v, P2V)

    loads[4].wait()
    arrived(g_all, GATHER)
    width = g_v.shape[1]
    total = dot(g_all[0], w_v[:, :width], (1, 1))
    for t in range(1, tp_size):
        total += dot(g_all[t], w_v[:, t * width : (t + 1) * width], (1, 1))
    do_v[...] = total.astype(BF16)

    def return_far(back, got, phase, dx):
        head = lax.rem(x + dx, NX)
        for dz in (0, 1, NZ - 1, 2, NZ - 2):
            slot = SLOT[((NZ - dz) % NZ, (NX - dx) % NX)]
            _, _, first, rows = SERVED[slot]
            src = back.at[:, head, pl.ds(pl.multiple_of(chunk_of(z + dz) + first, HALF), rows)]
            dst = got.at[slot, pl.ds(0, ENTRIES), pl.ds(first, rows)]
            if slot == 0:
                local(src, dst, phase)
            else:
                remote(src, dst, phase, (shard_at(dz, dx), tp))

    arrived(far_k, P2K)
    for dx in range(NX):
        head = lax.rem(x + dx, NX)
        lanes = lanes_of(head)
        pieces = []
        for a in range(BLK_DEV):
            rows = slice(a * BLK, (a + 1) * BLK)
            near = near_p[head, :, rows]
            keys = far_k[a * NREM : (a + 1) * NREM, head].reshape(NREM * BLK, D_HEAD)
            far = dot(keys, q_v[rows, lanes], (1, 1)) * SCALE
            count = live[me * BLK_DEV + a]
            entry = lax.broadcasted_iota(jnp.int32, far.shape, 0) // BLK
            far = jnp.where(entry < count, far, -1e30)
            highest = jnp.maximum(jnp.max(near, axis=0, keepdims=True), jnp.max(far, axis=0, keepdims=True))
            near = jnp.exp(near - highest)
            far = jnp.exp(far - highest)
            scale = 1.0 / (jnp.sum(near, axis=0, keepdims=True) + jnp.sum(far, axis=0, keepdims=True))
            near = near * scale
            far = far * scale
            near_p[head, :, rows] = near
            far_p[head, a] = far
            far_dv = dot(far.astype(BF16), do_v[rows, lanes], (1, 0)).astype(BF16)
            back_v[a * NREM : (a + 1) * NREM, head] = far_dv.reshape(NREM, BLK, D_HEAD)
            pieces.append(near.astype(BF16))
        return_far(back_v, got_v, R1V, dx)
        near_dv[head] = dot(jnp.concatenate(pieces, axis=1), do_v[:, lanes], (1, 0))

    arrived(far_v, P2V)
    for dx in range(NX):
        head = lax.rem(x + dx, NX)
        lanes = lanes_of(head)
        values = v_v[:, :, lanes].reshape(BLK_DEV * BLK, D_HEAD)
        near_grad = dot(values, do_v[:, lanes], (1, 1))
        pieces, fars = [], []
        for a in range(BLK_DEV):
            rows = slice(a * BLK, (a + 1) * BLK)
            far_values = far_v[a * NREM : (a + 1) * NREM, head].reshape(NREM * BLK, D_HEAD)
            grad = dot(far_values, do_v[rows, lanes], (1, 1))
            near, far = near_p[head, :, rows], far_p[head, a]
            own = near_grad[:, rows]
            delta = jnp.sum(near * own, axis=0, keepdims=True) + jnp.sum(far * grad, axis=0, keepdims=True)
            near = (near * (own - delta) * SCALE).astype(BF16)
            far = (far * (grad - delta) * SCALE).astype(BF16)
            far_dk = dot(far, q_v[rows, lanes], (1, 0)).astype(BF16)
            back_k[a * NREM : (a + 1) * NREM, head] = far_dk.reshape(NREM, BLK, D_HEAD)
            pieces.append(near)
            fars.append(far)
        return_far(back_k, got_k, R1K, dx)
        near = jnp.concatenate(pieces, axis=1)
        near_dk[head] = dot(near, q_v[:, lanes], (1, 0))
        keys = k_v[:, :, lanes].reshape(BLK_DEV * BLK, D_HEAD)
        near_dq = dot(near, keys, (0, 0))
        for a in range(BLK_DEV):
            rows = slice(a * BLK, (a + 1) * BLK)
            keys = far_k[a * NREM : (a + 1) * NREM, head].reshape(NREM * BLK, D_HEAD)
            dq_ref[rows, lanes] = (near_dq[rows] + dot(fars[a], keys, (0, 0))).astype(BF16)

    served = [shard_at(dz, dx) * BLK_DEV for dz, dx, _, _ in SERVED]
    table.wait()
    zeros = jnp.zeros((CHUNK, D_HEAD), BF16)

    def collect(got, sums, fin, phase):
        def one_block(block, _):
            upper = jnp.zeros((HALF, D_HEAD), F32)
            lower = jnp.zeros((HALF, D_HEAD), F32)
            for i, (_, _, first, rows) in enumerate(SERVED):
                e = jnp.minimum(inverse[block, served[i]], inverse[block, served[i] + 1])
                if first == 0:
                    upper += got[i, e, :HALF].astype(F32)
                if first + rows == CHUNK:
                    lower += got[i, e, HALF:].astype(F32)
            sums[block, :HALF] = upper.astype(BF16)
            sums[block, HALF:] = lower.astype(BF16)
            return 0

        lax.fori_loop(0, NBLK, one_block, 0)
        dst = fin.at[lax.div(z, NX), x, :, pl.ds(chunk_of(z), CHUNK)]
        for dz, dx in others:
            shard = shard_at(dz, dx)
            remote(sums.at[pl.ds(shard * BLK_DEV, BLK_DEV)], dst, phase, (shard, tp))
        local(sums.at[my_blocks], dst, phase)

    counted = (pl.ds(0, FULL_SLOTS), pl.ds(0, ENTRIES))
    for i in range(len(SERVED)):
        got_v[i, ENTRIES] = zeros
        got_k[i, ENTRIES] = zeros
    arrived(got_v.at[counted], R1V)
    collect(got_v, sum_v, fin_v, R2V)
    arrived(got_k.at[counted], R1K)
    collect(got_k, sum_k, fin_k, R2K)

    def finish(near, fin, out):
        for head in range(NX):
            total = near[head]
            for copy in range(2):
                total += fin[copy, head].reshape(BLK_DEV * BLK, D_HEAD).astype(F32)
            out[:, head * D_HEAD : (head + 1) * D_HEAD] = total.astype(BF16)

    arrived(fin_v, R2V)
    finish(near_dv, fin_v, dv_ref)
    arrived(fin_k, R2K)
    finish(near_dk, fin_k, dk_ref)

    most = pl.ds(0, NBLK - BLK_DEV)
    sent(hold_k.at[most], P1K)
    sent(hold_v.at[most], P1V)
    sent(g_all.at[pl.ds(0, tp_size - 1)], GATHER)
    fewer = (pl.ds(0, FULL_SLOTS - 1), pl.ds(0, ENTRIES))
    sent(pick_k.at[fewer], P2K)
    sent(pick_v.at[fewer], P2V)
    sent(got_v.at[fewer], R1V)
    sent(got_k.at[fewer], R1K)
    sent(sum_v.at[most], R2V)
    sent(sum_k.at[most], R2K)


def write_out(a_ref, b_ref, c_ref, a_out, b_out, c_out, held, taken, put):
    pairs = ((a_ref, a_out), (b_ref, b_out), (c_ref, c_out))
    takes = [pltpu.make_async_copy(src, held.at[i], taken.at[i]) for i, (src, _) in enumerate(pairs)]
    puts = [pltpu.make_async_copy(held.at[i], dst, put.at[i]) for i, (_, dst) in enumerate(pairs)]
    for copy in takes:
        copy.start()
    for take, copy in zip(takes, puts):
        take.wait()
        copy.start()
    for copy in puts:
        copy.wait()


def shards(tp_size, grad_out, out_weight, queries, keys, values, visible, live):
    rows, features = queries.shape
    heads = features // D_HEAD
    listed = visible.astype(jnp.int32).T
    smem = pl.BlockSpec(memory_space=pltpu.SMEM)
    anywhere = pl.BlockSpec(memory_space=pltpu.HBM)
    vmem = pl.BlockSpec(memory_space=pltpu.VMEM)
    out = jax.ShapeDtypeStruct((rows, features), BF16)
    tiles = pltpu.VMEM((NBLK, CHUNK, D_HEAD), BF16)
    picked = pltpu.VMEM((len(SERVED), ENTRIES, CHUNK, D_HEAD), BF16)
    far = pltpu.VMEM((ENTRIES, heads, BLK, D_HEAD), BF16)
    got = pltpu.VMEM((len(SERVED), ENTRIES + 1, CHUNK, D_HEAD), BF16)
    fin = pltpu.VMEM((2, heads, BLK_DEV, BLK, D_HEAD), BF16)
    near = pltpu.VMEM((heads, rows, D_HEAD), F32)
    split = (BLK_DEV, BLK, features)
    outs = pl.pallas_call(
        functools.partial(kernel, tp_size),
        out_shape=(out, out, out),
        in_specs=[smem, smem, vmem] + [anywhere] * 5,
        out_specs=(vmem, vmem, vmem),
        scratch_shapes=[
            pltpu.VMEM(grad_out.shape, BF16),
            pltpu.VMEM(out_weight.shape, BF16),
            pltpu.VMEM(queries.shape, BF16),
            pltpu.VMEM(split, BF16),
            pltpu.VMEM(split, BF16),
            pltpu.VMEM((tp_size,) + grad_out.shape, BF16),
            pltpu.VMEM(queries.shape, BF16),
            tiles, tiles, picked, picked, far, far,
            far, far, got, got, tiles, tiles, fin, fin,
            pltpu.VMEM((heads, rows, rows), F32),
            pltpu.VMEM((heads, BLK_DEV, NREM * BLK, BLK), F32),
            near, near,
            pltpu.VMEM((NBLK, NBLK), jnp.int32),
            pltpu.SMEM((NBLK, NBLK), jnp.int32),
            pltpu.SemaphoreType.DMA((9,)),
            pltpu.SemaphoreType.DMA((9,)),
            pltpu.SemaphoreType.DMA((6,)),
        ],
        compiler_params=pltpu.CompilerParams(
            collective_id=0, has_side_effects=True, vmem_limit_bytes=56 * 2**20
        ),
    )(
        listed, live, listed,
        grad_out, out_weight, queries, keys.reshape(split), values.reshape(split),
    )
    return pl.pallas_call(
        write_out,
        out_shape=(out, out, out),
        in_specs=[anywhere] * 3,
        out_specs=(anywhere,) * 3,
        scratch_shapes=[
            pltpu.VMEM((3, rows, features), BF16),
            pltpu.SemaphoreType.DMA((3,)),
            pltpu.SemaphoreType.DMA((3,)),
        ],
    )(*outs)


def solution(mesh):
    placed = (
        P("seq", "tp"),
        P("tp", None),
        P("seq", "tp"),
        P("seq", "tp"),
        P("seq", "tp"),
        P(),
        P(),
    )
    return jax.shard_map(
        functools.partial(shards, mesh.shape["tp"]),
        mesh=mesh,
        in_specs=placed,
        out_specs=(P("seq", "tp"), P("seq", "tp"), P("seq", "tp")),
        check_vma=False,
    )
```

```python
import functools
import math

import jax
import jax.numpy as jnp
from jax import lax
from jax.experimental import pallas as pl
from jax.experimental.pallas import tpu as pltpu
from jax.sharding import PartitionSpec as P

MESH = pl.DeviceIdType.MESH
BF16 = jnp.bfloat16
F32 = jnp.float32

D_HEAD = 128
BLK = 128
BLK_DEV = 2
NREM = 3
ENTRIES = BLK_DEV * NREM
NZ, NX = 8, 4
SHARDS = NZ * NX
NBLK = SHARDS * BLK_DEV
CHUNK = 32
HALF = CHUNK // 2
SCALE = 1.0 / math.sqrt(D_HEAD)

SERVED = (
    [(dz, dx, 0, CHUNK) for dz in (0, 1, NZ - 1) for dx in range(NX)]
    + [(2, dx, HALF, HALF) for dx in range(NX)]
    + [(NZ - 2, dx, 0, HALF) for dx in range(NX)]
)
SLOT = {(dz, dx): i for i, (dz, dx, _, _) in enumerate(SERVED)}
FULL_SLOTS = 16

P1K, P1V, P2K, P2V, R1V, R1K, R2V, R2K, GATHER = range(9)


def dot(a, b, contract):
    return lax.dot_general(a, b, ((contract[:1], contract[1:]), ((), ())), preferred_element_type=F32)


def add_terms(near, fin, out):
    for head in range(NX):
        total = near[head]
        for copy in range(2):
            total += fin[copy, head].reshape(BLK_DEV * BLK, D_HEAD).astype(F32)
        out[:, head * D_HEAD : (head + 1) * D_HEAD] = total.astype(BF16)


def kernel(
    tp_size,
    visible, live, listed,
    g_hbm, w_hbm, q_hbm, k_hbm, v_hbm,
    dq_hbm, dv_hbm, near_dk_hbm, fin_k,
    g_v, w_v, q_v, k_v, v_v, g_all, do_v,
    hold_k, hold_v, pick_k, pick_v, far_k, far_v,
    back_v, back_k, got_v, got_k, sum_v, sum_k, fin_v,
    dq_ref, dv_ref, near_p, far_p, near_dv, near_dk, found, inverse,
    send, recv, load, store,
):
    me = lax.axis_index("seq")
    tp = lax.axis_index("tp")
    z, x = lax.div(me, NX), lax.rem(me, NX)
    others = [(dz, dx) for dz in range(NZ) for dx in range(NX) if (dz, dx) != (0, 0)]

    def shard_at(dz, dx):
        return lax.rem(z + dz, NZ) * NX + lax.rem(x + dx, NX)

    barrier = pltpu.get_barrier_semaphore()
    for dz, dx in others:
        pl.semaphore_signal(barrier, inc=1, device_id=(shard_at(dz, dx), tp), device_id_type=MESH)
    for dt in range(1, tp_size):
        pl.semaphore_signal(barrier, inc=1, device_id=(me, lax.rem(tp + dt, tp_size)), device_id_type=MESH)
    loads = [
        pltpu.make_async_copy(src, dst, load.at[i])
        for i, (src, dst) in enumerate(((k_hbm, k_v), (g_hbm, g_v), (v_hbm, v_v), (q_hbm, q_v), (w_hbm, w_v)))
    ]
    for copy in loads:
        copy.start()
    shape = (NBLK, NBLK)
    block = lax.broadcasted_iota(jnp.int32, shape, 0)
    first_entry = lax.broadcasted_iota(jnp.int32, shape, 1) % BLK_DEV * NREM
    place = jnp.full(shape, ENTRIES, jnp.int32)
    for j in range(NREM):
        place = jnp.where(listed[j : j + 1, :] == block, first_entry + j, place)
    found[...] = place
    table = pltpu.make_async_copy(found, inverse, load.at[5])
    table.start()
    loads[0].wait()
    loads[1].wait()
    loads[2].wait()
    pl.semaphore_wait(barrier, len(others) + tp_size - 1)

    def remote(src, dst, phase, device):
        pltpu.make_async_remote_copy(
            src_ref=src, dst_ref=dst, send_sem=send.at[phase], recv_sem=recv.at[phase],
            device_id=device, device_id_type=MESH,
        ).start()

    def local(src, dst, phase):
        pltpu.make_async_copy(src, dst, recv.at[phase]).start()

    def arrived(ref, phase):
        pltpu.make_async_copy(ref, ref, recv.at[phase]).wait()

    def sent(ref, phase):
        pltpu.make_async_copy(ref, ref, send.at[phase]).wait()

    def chunk_of(zz):
        return pl.multiple_of(lax.rem(zz, NX) * CHUNK, CHUNK)

    def lanes_of(head):
        return pl.ds(pl.multiple_of(head * D_HEAD, D_HEAD), D_HEAD)

    my_blocks = pl.ds(me * BLK_DEV, BLK_DEV)

    def spread(own, hold, phase):
        def part(dz, dx):
            return own.at[:, pl.ds(chunk_of(z + dz), CHUNK), lanes_of(lax.rem(x + dx, NX))]

        for dz, dx in others:
            remote(part(dz, dx), hold.at[my_blocks], phase, (shard_at(dz, dx), tp))
        local(part(0, 0), hold.at[my_blocks], phase)

    spread(k_v, hold_k, P1K)
    for dt in range(1, tp_size):
        remote(g_v, g_all.at[tp], GATHER, (me, lax.rem(tp + dt, tp_size)))
    local(g_v, g_all.at[tp], GATHER)
    spread(v_v, hold_v, P1V)

    loads[3].wait()

    def near_scores(head, _):
        lanes = lanes_of(head)
        keys = k_v[:, :, lanes].reshape(BLK_DEV * BLK, D_HEAD)
        near_p[head] = dot(keys, q_v[:, lanes], (1, 1)) * SCALE
        return 0

    lax.fori_loop(0, NX, near_scores, 0)

    def forward(hold, pick, far, phase):
        for i, (dz, dx, first, rows) in enumerate(SERVED):
            shard = shard_at(dz, dx)
            for e in range(ENTRIES):
                block = visible[e % NREM, shard * BLK_DEV + e // NREM]
                pick[i, e, first : first + rows] = hold[block, first : first + rows]
        for i, (dz, dx, first, rows) in enumerate(SERVED):
            src = pick.at[i, :, pl.ds(first, rows)]
            dst = far.at[:, x, pl.ds(pl.multiple_of(chunk_of(z) + first, HALF), rows)]
            if i == 0:
                local(src, dst, phase)
            else:
                remote(src, dst, phase, (shard_at(dz, dx), tp))

    arrived(hold_k, P1K)
    forward(hold_k, pick_k, far_k, P2K)
    arrived(hold_v, P1V)
    forward(hold_v, pick_v, far_v, P2V)

    loads[4].wait()
    arrived(g_all, GATHER)
    width = g_v.shape[1]
    total = dot(g_all[0], w_v[:, :width], (1, 1))
    for t in range(1, tp_size):
        total += dot(g_all[t], w_v[:, t * width : (t + 1) * width], (1, 1))
    do_v[...] = total.astype(BF16)

    def return_far(back, got, phase, dx):
        head = lax.rem(x + dx, NX)
        for dz in (0, 1, NZ - 1, 2, NZ - 2):
            slot = SLOT[((NZ - dz) % NZ, (NX - dx) % NX)]
            _, _, first, rows = SERVED[slot]
            src = back.at[:, head, pl.ds(pl.multiple_of(chunk_of(z + dz) + first, HALF), rows)]
            dst = got.at[slot, pl.ds(0, ENTRIES), pl.ds(first, rows)]
            if slot == 0:
                local(src, dst, phase)
            else:
                remote(src, dst, phase, (shard_at(dz, dx), tp))

    arrived(far_k, P2K)
    for dx in range(NX):
        head = lax.rem(x + dx, NX)
        lanes = lanes_of(head)
        pieces = []
        for a in range(BLK_DEV):
            rows = slice(a * BLK, (a + 1) * BLK)
            near = near_p[head, :, rows]
            keys = far_k[a * NREM : (a + 1) * NREM, head].reshape(NREM * BLK, D_HEAD)
            far = dot(keys, q_v[rows, lanes], (1, 1)) * SCALE
            count = live[me * BLK_DEV + a]
            entry = lax.broadcasted_iota(jnp.int32, far.shape, 0) // BLK
            far = jnp.where(entry < count, far, -1e30)
            highest = jnp.maximum(jnp.max(near, axis=0, keepdims=True), jnp.max(far, axis=0, keepdims=True))
            near = jnp.exp(near - highest)
            far = jnp.exp(far - highest)
            scale = 1.0 / (jnp.sum(near, axis=0, keepdims=True) + jnp.sum(far, axis=0, keepdims=True))
            near = near * scale
            far = far * scale
            near_p[head, :, rows] = near
            far_p[head, a] = far
            far_dv = dot(far.astype(BF16), do_v[rows, lanes], (1, 0)).astype(BF16)
            back_v[a * NREM : (a + 1) * NREM, head] = far_dv.reshape(NREM, BLK, D_HEAD)
            pieces.append(near.astype(BF16))
        return_far(back_v, got_v, R1V, dx)
        near_dv[head] = dot(jnp.concatenate(pieces, axis=1), do_v[:, lanes], (1, 0))

    arrived(far_v, P2V)
    for dx in range(NX):
        head = lax.rem(x + dx, NX)
        lanes = lanes_of(head)
        values = v_v[:, :, lanes].reshape(BLK_DEV * BLK, D_HEAD)
        near_grad = dot(values, do_v[:, lanes], (1, 1))
        pieces, fars = [], []
        for a in range(BLK_DEV):
            rows = slice(a * BLK, (a + 1) * BLK)
            far_values = far_v[a * NREM : (a + 1) * NREM, head].reshape(NREM * BLK, D_HEAD)
            grad = dot(far_values, do_v[rows, lanes], (1, 1))
            near, far = near_p[head, :, rows], far_p[head, a]
            own = near_grad[:, rows]
            delta = jnp.sum(near * own, axis=0, keepdims=True) + jnp.sum(far * grad, axis=0, keepdims=True)
            near = (near * (own - delta) * SCALE).astype(BF16)
            far = (far * (grad - delta) * SCALE).astype(BF16)
            far_dk = dot(far, q_v[rows, lanes], (1, 0)).astype(BF16)
            back_k[a * NREM : (a + 1) * NREM, head] = far_dk.reshape(NREM, BLK, D_HEAD)
            pieces.append(near)
            fars.append(far)
        return_far(back_k, got_k, R1K, dx)
        near = jnp.concatenate(pieces, axis=1)
        near_dk[head] = dot(near, q_v[:, lanes], (1, 0))
        keys = k_v[:, :, lanes].reshape(BLK_DEV * BLK, D_HEAD)
        near_dq = dot(near, keys, (0, 0))
        for a in range(BLK_DEV):
            rows = slice(a * BLK, (a + 1) * BLK)
            keys = far_k[a * NREM : (a + 1) * NREM, head].reshape(NREM * BLK, D_HEAD)
            dq_ref[rows, lanes] = (near_dq[rows] + dot(fars[a], keys, (0, 0))).astype(BF16)

    stores = [
        pltpu.make_async_copy(src, dst, store.at[i])
        for i, (src, dst) in enumerate(((dq_ref, dq_hbm), (near_dk, near_dk_hbm), (dv_ref, dv_hbm)))
    ]
    stores[0].start()
    stores[1].start()

    served = [shard_at(dz, dx) * BLK_DEV for dz, dx, _, _ in SERVED]
    table.wait()
    zeros = jnp.zeros((CHUNK, D_HEAD), BF16)

    def collect(got, sums, fin, phase):
        def one_block(block, _):
            upper = jnp.zeros((HALF, D_HEAD), F32)
            lower = jnp.zeros((HALF, D_HEAD), F32)
            for i, (_, _, first, rows) in enumerate(SERVED):
                e = jnp.minimum(inverse[block, served[i]], inverse[block, served[i] + 1])
                if first == 0:
                    upper += got[i, e, :HALF].astype(F32)
                if first + rows == CHUNK:
                    lower += got[i, e, HALF:].astype(F32)
            sums[block, :HALF] = upper.astype(BF16)
            sums[block, HALF:] = lower.astype(BF16)
            return 0

        lax.fori_loop(0, NBLK, one_block, 0)
        dst = fin.at[lax.div(z, NX), x, :, pl.ds(chunk_of(z), CHUNK)]
        for dz, dx in others:
            shard = shard_at(dz, dx)
            remote(sums.at[pl.ds(shard * BLK_DEV, BLK_DEV)], dst, phase, (shard, tp))
        local(sums.at[my_blocks], dst, phase)

    counted = (pl.ds(0, FULL_SLOTS), pl.ds(0, ENTRIES))
    for i in range(len(SERVED)):
        got_v[i, ENTRIES] = zeros
        got_k[i, ENTRIES] = zeros
    arrived(got_v.at[counted], R1V)
    collect(got_v, sum_v, fin_v, R2V)
    arrived(got_k.at[counted], R1K)
    collect(got_k, sum_k, fin_k, R2K)

    arrived(fin_v, R2V)
    add_terms(near_dv, fin_v, dv_ref)
    stores[2].start()
    for copy in stores:
        copy.wait()

    most = pl.ds(0, NBLK - BLK_DEV)
    sent(hold_k.at[most], P1K)
    sent(hold_v.at[most], P1V)
    sent(g_all.at[pl.ds(0, tp_size - 1)], GATHER)
    fewer = (pl.ds(0, FULL_SLOTS - 1), pl.ds(0, ENTRIES))
    sent(pick_k.at[fewer], P2K)
    sent(pick_v.at[fewer], P2V)
    sent(got_v.at[fewer], R1V)
    sent(got_k.at[fewer], R1K)
    sent(sum_v.at[most], R2V)
    sent(sum_k.at[most], R2K)
    arrived(fin_k, R2K)


def write_out(dq, dv, near_dk, fin_k, dq_out, dk_out, dv_out, dq_v, dv_v, near_v, fin_v, dk_v, taken, put):
    sources = ((near_dk, near_v), (fin_k, fin_v), (dq, dq_v), (dv, dv_v))
    takes = [pltpu.make_async_copy(src, dst, taken.at[i]) for i, (src, dst) in enumerate(sources)]
    results = ((dq_v, dq_out), (dv_v, dv_out), (dk_v, dk_out))
    puts = [pltpu.make_async_copy(src, dst, put.at[i]) for i, (src, dst) in enumerate(results)]
    for copy in takes:
        copy.start()
    takes[2].wait()
    puts[0].start()
    takes[3].wait()
    puts[1].start()
    takes[0].wait()
    takes[1].wait()
    add_terms(near_v, fin_v, dk_v)
    puts[2].start()
    for copy in puts:
        copy.wait()


def shards(tp_size, grad_out, out_weight, queries, keys, values, visible, live):
    rows, features = queries.shape
    heads = features // D_HEAD
    listed = visible.astype(jnp.int32).T
    smem = pl.BlockSpec(memory_space=pltpu.SMEM)
    anywhere = pl.BlockSpec(memory_space=pltpu.HBM)
    vmem = pl.BlockSpec(memory_space=pltpu.VMEM)
    out = jax.ShapeDtypeStruct((rows, features), BF16)
    tiles = pltpu.VMEM((NBLK, CHUNK, D_HEAD), BF16)
    picked = pltpu.VMEM((len(SERVED), ENTRIES, CHUNK, D_HEAD), BF16)
    far = pltpu.VMEM((ENTRIES, heads, BLK, D_HEAD), BF16)
    got = pltpu.VMEM((len(SERVED), ENTRIES + 1, CHUNK, D_HEAD), BF16)
    fin = pltpu.VMEM((2, heads, BLK_DEV, BLK, D_HEAD), BF16)
    near = pltpu.VMEM((heads, rows, D_HEAD), F32)
    split = (BLK_DEV, BLK, features)
    near_out = jax.ShapeDtypeStruct((heads, rows, D_HEAD), F32)
    fin_out = jax.ShapeDtypeStruct((2, heads, BLK_DEV, BLK, D_HEAD), BF16)
    outs = pl.pallas_call(
        functools.partial(kernel, tp_size),
        out_shape=(out, out, near_out, fin_out),
        in_specs=[smem, smem, vmem] + [anywhere] * 5,
        out_specs=(anywhere,) * 4,
        scratch_shapes=[
            pltpu.VMEM(grad_out.shape, BF16),
            pltpu.VMEM(out_weight.shape, BF16),
            pltpu.VMEM(queries.shape, BF16),
            pltpu.VMEM(split, BF16),
            pltpu.VMEM(split, BF16),
            pltpu.VMEM((tp_size,) + grad_out.shape, BF16),
            pltpu.VMEM(queries.shape, BF16),
            tiles, tiles, picked, picked, far, far,
            far, far, got, got, tiles, tiles, fin,
            pltpu.VMEM(queries.shape, BF16),
            pltpu.VMEM(queries.shape, BF16),
            pltpu.VMEM((heads, rows, rows), F32),
            pltpu.VMEM((heads, BLK_DEV, NREM * BLK, BLK), F32),
            near, near,
            pltpu.VMEM((NBLK, NBLK), jnp.int32),
            pltpu.SMEM((NBLK, NBLK), jnp.int32),
            pltpu.SemaphoreType.DMA((9,)),
            pltpu.SemaphoreType.DMA((9,)),
            pltpu.SemaphoreType.DMA((6,)),
            pltpu.SemaphoreType.DMA((3,)),
        ],
        compiler_params=pltpu.CompilerParams(
            collective_id=0, has_side_effects=True, vmem_limit_bytes=56 * 2**20
        ),
    )(
        listed, live, listed,
        grad_out, out_weight, queries, keys.reshape(split), values.reshape(split),
    )
    return pl.pallas_call(
        write_out,
        out_shape=(out, out, out),
        in_specs=[anywhere] * 4,
        out_specs=(anywhere,) * 3,
        scratch_shapes=[
            pltpu.VMEM(queries.shape, BF16),
            pltpu.VMEM(queries.shape, BF16),
            near, fin,
            pltpu.VMEM(queries.shape, BF16),
            pltpu.SemaphoreType.DMA((4,)),
            pltpu.SemaphoreType.DMA((3,)),
        ],
    )(*outs)


def solution(mesh):
    placed = (
        P("seq", "tp"),
        P("tp", None),
        P("seq", "tp"),
        P("seq", "tp"),
        P("seq", "tp"),
        P(),
        P(),
    )
    return jax.shard_map(
        functools.partial(shards, mesh.shape["tp"]),
        mesh=mesh,
        in_specs=placed,
        out_specs=(P("seq", "tp"), P("seq", "tp"), P("seq", "tp")),
        check_vma=False,
    )
```

```python
import functools
import math

import jax
import jax.numpy as jnp
from jax import lax
from jax.experimental import pallas as pl
from jax.experimental.pallas import tpu as pltpu
from jax.sharding import PartitionSpec as P

MESH = pl.DeviceIdType.MESH
BF16 = jnp.bfloat16
F32 = jnp.float32

D_HEAD = 128
BLK = 128
BLK_DEV = 2
NREM = 3
ENTRIES = BLK_DEV * NREM
NZ, NX = 8, 4
SHARDS = NZ * NX
NBLK = SHARDS * BLK_DEV
CHUNK = 32
HALF = CHUNK // 2
SCALE = 1.0 / math.sqrt(D_HEAD)

SERVED = (
    [(dz, dx, 0, CHUNK) for dz in (0, 1, NZ - 1) for dx in range(NX)]
    + [(2, dx, HALF, HALF) for dx in range(NX)]
    + [(NZ - 2, dx, 0, HALF) for dx in range(NX)]
)
SLOT = {(dz, dx): i for i, (dz, dx, _, _) in enumerate(SERVED)}
FULL_SLOTS = 16

P1K, P1V, P2K, P2V, R1V, R1K, R2V, R2K, GATHER = range(9)


def dot(a, b, contract):
    return lax.dot_general(a, b, ((contract[:1], contract[1:]), ((), ())), preferred_element_type=F32)


def add_terms(near, fin, out, head):
    total = near[head]
    for copy in range(2):
        total += fin[copy, head].reshape(BLK_DEV * BLK, D_HEAD).astype(F32)
    out[:, head * D_HEAD : (head + 1) * D_HEAD] = total.astype(BF16)


def kernel(
    tp_size,
    visible, live, listed,
    g_hbm, w_hbm, q_hbm, k_hbm, v_hbm,
    dq_hbm, dv_hbm, near_dk_hbm, fin_k,
    g_v, w_v, q_v, k_v, v_v, g_all, do_v,
    hold_k, hold_v, pick_k, pick_v, far_k, far_v,
    back_v, back_k, got_v, got_k, sum_v, sum_k, fin_v,
    dq_ref, dv_ref, near_p, far_p, near_dv, near_dk, found, inverse,
    send, recv, load, store, upward, downward,
):
    me = lax.axis_index("seq")
    tp = lax.axis_index("tp")
    z, x = lax.div(me, NX), lax.rem(me, NX)
    others = [(dz, dx) for dz in range(NZ) for dx in range(NX) if (dz, dx) != (0, 0)]

    def shard_at(dz, dx):
        return lax.rem(z + dz, NZ) * NX + lax.rem(x + dx, NX)

    barrier = pltpu.get_barrier_semaphore()
    greeted = [(1, 0), (NZ - 1, 0)] + [(0, dx) for dx in range(1, NX)]
    for dz, dx in greeted:
        pl.semaphore_signal(barrier, inc=1, device_id=(shard_at(dz, dx), tp), device_id_type=MESH)
    for dt in range(1, tp_size):
        pl.semaphore_signal(barrier, inc=1, device_id=(me, lax.rem(tp + dt, tp_size)), device_id_type=MESH)
    loads = [
        pltpu.make_async_copy(src, dst, load.at[i])
        for i, (src, dst) in enumerate(((k_hbm, k_v), (g_hbm, g_v), (v_hbm, v_v), (q_hbm, q_v), (w_hbm, w_v)))
    ]
    for copy in loads:
        copy.start()
    shape = (NBLK, NBLK)
    block = lax.broadcasted_iota(jnp.int32, shape, 0)
    first_entry = lax.broadcasted_iota(jnp.int32, shape, 1) % BLK_DEV * NREM
    place = jnp.full(shape, ENTRIES, jnp.int32)
    for j in range(NREM):
        place = jnp.where(listed[j : j + 1, :] == block, first_entry + j, place)
    found[...] = place
    table = pltpu.make_async_copy(found, inverse, load.at[5])
    table.start()
    loads[0].wait()
    loads[1].wait()
    loads[2].wait()
    pl.semaphore_wait(barrier, len(greeted) + tp_size - 1)

    def remote(src, dst, phase, device):
        pltpu.make_async_remote_copy(
            src_ref=src, dst_ref=dst, send_sem=send.at[phase], recv_sem=recv.at[phase],
            device_id=device, device_id_type=MESH,
        ).start()

    def local(src, dst, phase):
        pltpu.make_async_copy(src, dst, recv.at[phase]).start()

    def arrived(ref, phase):
        pltpu.make_async_copy(ref, ref, recv.at[phase]).wait()

    def sent(ref, phase):
        pltpu.make_async_copy(ref, ref, send.at[phase]).wait()

    def chunk_of(zz):
        return pl.multiple_of(lax.rem(zz, NX) * CHUNK, CHUNK)

    def lanes_of(head):
        return pl.ds(pl.multiple_of(head * D_HEAD, D_HEAD), D_HEAD)

    my_blocks = pl.ds(me * BLK_DEV, BLK_DEV)

    def spread(own, hold, phase, dz):
        for dx in range(NX):
            src = own.at[:, pl.ds(chunk_of(z + dz), CHUNK), lanes_of(lax.rem(x + dx, NX))]
            if (dz, dx) == (0, 0):
                local(src, hold.at[my_blocks], phase)
            else:
                remote(src, hold.at[my_blocks], phase, (shard_at(dz, dx), tp))

    def tell(semaphore, dz):
        pl.semaphore_signal(semaphore, inc=1, device_id=(shard_at(dz, 0), tp), device_id_type=MESH)

    tell(upward, NZ - 1)
    tell(downward, 1)
    spread(k_v, hold_k, P1K, 0)
    half = NZ // 2
    for step in range(1, half + 1):
        pl.semaphore_wait(upward, 1)
        if step < half:
            tell(upward, NZ - 1)
        spread(k_v, hold_k, P1K, step)
        if step < half:
            pl.semaphore_wait(downward, 1)
            if step < half - 1:
                tell(downward, 1)
            spread(k_v, hold_k, P1K, NZ - step)
            if step == 2:
                spread(v_v, hold_v, P1V, 0)
                spread(v_v, hold_v, P1V, 1)
                spread(v_v, hold_v, P1V, NZ - 1)
    for dt in range(1, tp_size):
        remote(g_v, g_all.at[tp], GATHER, (me, lax.rem(tp + dt, tp_size)))
    local(g_v, g_all.at[tp], GATHER)
    for dz in range(2, NZ - 1):
        spread(v_v, hold_v, P1V, dz)

    loads[3].wait()

    def near_scores(head, _):
        lanes = lanes_of(head)
        keys = k_v[:, :, lanes].reshape(BLK_DEV * BLK, D_HEAD)
        near_p[head] = dot(keys, q_v[:, lanes], (1, 1)) * SCALE
        return 0

    lax.fori_loop(0, NX, near_scores, 0)

    def forward(hold, pick, far, phase):
        for i, (dz, dx, first, rows) in enumerate(SERVED):
            shard = shard_at(dz, dx)
            for e in range(ENTRIES):
                block = visible[e % NREM, shard * BLK_DEV + e // NREM]
                pick[i, e, first : first + rows] = hold[block, first : first + rows]
        for i, (dz, dx, first, rows) in enumerate(SERVED):
            src = pick.at[i, :, pl.ds(first, rows)]
            dst = far.at[:, x, pl.ds(pl.multiple_of(chunk_of(z) + first, HALF), rows)]
            if i == 0:
                local(src, dst, phase)
            else:
                remote(src, dst, phase, (shard_at(dz, dx), tp))

    arrived(hold_k, P1K)
    forward(hold_k, pick_k, far_k, P2K)
    arrived(hold_v, P1V)
    forward(hold_v, pick_v, far_v, P2V)

    loads[4].wait()
    arrived(g_all, GATHER)
    width = g_v.shape[1]
    total = dot(g_all[0], w_v[:, :width], (1, 1))
    for t in range(1, tp_size):
        total += dot(g_all[t], w_v[:, t * width : (t + 1) * width], (1, 1))
    do_v[...] = total.astype(BF16)

    def return_far(back, got, phase, dx):
        head = lax.rem(x + dx, NX)
        for dz in (0, 1, NZ - 1, 2, NZ - 2):
            slot = SLOT[((NZ - dz) % NZ, (NX - dx) % NX)]
            _, _, first, rows = SERVED[slot]
            src = back.at[:, head, pl.ds(pl.multiple_of(chunk_of(z + dz) + first, HALF), rows)]
            dst = got.at[slot, pl.ds(0, ENTRIES), pl.ds(first, rows)]
            if slot == 0:
                local(src, dst, phase)
            else:
                remote(src, dst, phase, (shard_at(dz, dx), tp))

    arrived(far_k, P2K)
    for dx in range(NX):
        head = lax.rem(x + dx, NX)
        lanes = lanes_of(head)
        pieces = []
        for a in range(BLK_DEV):
            rows = slice(a * BLK, (a + 1) * BLK)
            near = near_p[head, :, rows]
            keys = far_k[a * NREM : (a + 1) * NREM, head].reshape(NREM * BLK, D_HEAD)
            far = dot(keys, q_v[rows, lanes], (1, 1)) * SCALE
            count = live[me * BLK_DEV + a]
            entry = lax.broadcasted_iota(jnp.int32, far.shape, 0) // BLK
            far = jnp.where(entry < count, far, -1e30)
            highest = jnp.maximum(jnp.max(near, axis=0, keepdims=True), jnp.max(far, axis=0, keepdims=True))
            near = jnp.exp(near - highest)
            far = jnp.exp(far - highest)
            scale = 1.0 / (jnp.sum(near, axis=0, keepdims=True) + jnp.sum(far, axis=0, keepdims=True))
            near = near * scale
            far = far * scale
            near_p[head, :, rows] = near
            far_p[head, a] = far
            far_dv = dot(far.astype(BF16), do_v[rows, lanes], (1, 0)).astype(BF16)
            back_v[a * NREM : (a + 1) * NREM, head] = far_dv.reshape(NREM, BLK, D_HEAD)
            pieces.append(near.astype(BF16))
        return_far(back_v, got_v, R1V, dx)
        near_dv[head] = dot(jnp.concatenate(pieces, axis=1), do_v[:, lanes], (1, 0))

    arrived(far_v, P2V)
    for dx in range(NX):
        head = lax.rem(x + dx, NX)
        lanes = lanes_of(head)
        values = v_v[:, :, lanes].reshape(BLK_DEV * BLK, D_HEAD)
        near_grad = dot(values, do_v[:, lanes], (1, 1))
        pieces, fars = [], []
        for a in range(BLK_DEV):
            rows = slice(a * BLK, (a + 1) * BLK)
            far_values = far_v[a * NREM : (a + 1) * NREM, head].reshape(NREM * BLK, D_HEAD)
            grad = dot(far_values, do_v[rows, lanes], (1, 1))
            near, far = near_p[head, :, rows], far_p[head, a]
            own = near_grad[:, rows]
            delta = jnp.sum(near * own, axis=0, keepdims=True) + jnp.sum(far * grad, axis=0, keepdims=True)
            near = (near * (own - delta) * SCALE).astype(BF16)
            far = (far * (grad - delta) * SCALE).astype(BF16)
            far_dk = dot(far, q_v[rows, lanes], (1, 0)).astype(BF16)
            back_k[a * NREM : (a + 1) * NREM, head] = far_dk.reshape(NREM, BLK, D_HEAD)
            pieces.append(near)
            fars.append(far)
        return_far(back_k, got_k, R1K, dx)
        near = jnp.concatenate(pieces, axis=1)
        near_dk[head] = dot(near, q_v[:, lanes], (1, 0))
        keys = k_v[:, :, lanes].reshape(BLK_DEV * BLK, D_HEAD)
        near_dq = dot(near, keys, (0, 0))
        for a in range(BLK_DEV):
            rows = slice(a * BLK, (a + 1) * BLK)
            keys = far_k[a * NREM : (a + 1) * NREM, head].reshape(NREM * BLK, D_HEAD)
            dq_ref[rows, lanes] = (near_dq[rows] + dot(fars[a], keys, (0, 0))).astype(BF16)

    stores = [
        pltpu.make_async_copy(src, dst, store.at[i])
        for i, (src, dst) in enumerate(((dq_ref, dq_hbm), (near_dk, near_dk_hbm), (dv_ref, dv_hbm)))
    ]
    stores[0].start()
    stores[1].start()

    served = [shard_at(dz, dx) * BLK_DEV for dz, dx, _, _ in SERVED]
    table.wait()
    zeros = jnp.zeros((CHUNK, D_HEAD), BF16)

    def collect(got, sums, fin, phase):
        def one_block(block, _):
            upper = jnp.zeros((HALF, D_HEAD), F32)
            lower = jnp.zeros((HALF, D_HEAD), F32)
            for i, (_, _, first, rows) in enumerate(SERVED):
                e = jnp.minimum(inverse[block, served[i]], inverse[block, served[i] + 1])
                if first == 0:
                    upper += got[i, e, :HALF].astype(F32)
                if first + rows == CHUNK:
                    lower += got[i, e, HALF:].astype(F32)
            sums[block, :HALF] = upper.astype(BF16)
            sums[block, HALF:] = lower.astype(BF16)
            return 0

        lax.fori_loop(0, NBLK, one_block, 0)
        dst = fin.at[lax.div(z, NX), x, :, pl.ds(chunk_of(z), CHUNK)]
        for dz, dx in others:
            shard = shard_at(dz, dx)
            remote(sums.at[pl.ds(shard * BLK_DEV, BLK_DEV)], dst, phase, (shard, tp))
        local(sums.at[my_blocks], dst, phase)

    counted = (pl.ds(0, FULL_SLOTS), pl.ds(0, ENTRIES))
    for i in range(len(SERVED)):
        got_v[i, ENTRIES] = zeros
        got_k[i, ENTRIES] = zeros
    arrived(got_v.at[counted], R1V)
    collect(got_v, sum_v, fin_v, R2V)
    arrived(got_k.at[counted], R1K)
    collect(got_k, sum_k, fin_k, R2K)

    arrived(fin_v, R2V)
    for head in range(NX):
        add_terms(near_dv, fin_v, dv_ref, head)
    stores[2].start()
    for copy in stores:
        copy.wait()

    most = pl.ds(0, NBLK - BLK_DEV)
    sent(hold_k.at[most], P1K)
    sent(hold_v.at[most], P1V)
    sent(g_all.at[pl.ds(0, tp_size - 1)], GATHER)
    fewer = (pl.ds(0, FULL_SLOTS - 1), pl.ds(0, ENTRIES))
    sent(pick_k.at[fewer], P2K)
    sent(pick_v.at[fewer], P2V)
    sent(got_v.at[fewer], R1V)
    sent(got_k.at[fewer], R1K)
    sent(sum_v.at[most], R2V)
    sent(sum_k.at[most], R2K)
    arrived(fin_k, R2K)


def write_out(dq, dv, near_dk, fin_k, dq_out, dk_out, dv_out, dq_v, dv_v, near_v, fin_v, dk_v, taken, put):
    heads = near_dk.shape[0]
    takes, puts = [], []
    for head in range(heads):
        lanes = pl.ds(head * D_HEAD, D_HEAD)
        takes.append((
            pltpu.make_async_copy(fin_k.at[:, head], fin_v.at[:, head], taken.at[2 * head]),
            pltpu.make_async_copy(near_dk.at[head], near_v.at[head], taken.at[2 * head + 1]),
        ))
        puts.append(pltpu.make_async_copy(dk_v.at[:, lanes], dk_out.at[:, lanes], put.at[head]))
    whole = ((dq, dq_v, dq_out), (dv, dv_v, dv_out))
    for i, (src, held, dst) in enumerate(whole):
        takes.append((pltpu.make_async_copy(src, held, taken.at[2 * heads + i]),))
        puts.append(pltpu.make_async_copy(held, dst, put.at[heads + i]))
    order = [heads, heads + 1] + list(range(heads))
    for i in order:
        for copy in takes[i]:
            copy.start()
    for i in order:
        for copy in takes[i]:
            copy.wait()
        if i < heads:
            add_terms(near_v, fin_v, dk_v, i)
        puts[i].start()
    for copy in puts:
        copy.wait()


def shards(tp_size, grad_out, out_weight, queries, keys, values, visible, live):
    rows, features = queries.shape
    heads = features // D_HEAD
    listed = visible.astype(jnp.int32).T
    smem = pl.BlockSpec(memory_space=pltpu.SMEM)
    anywhere = pl.BlockSpec(memory_space=pltpu.HBM)
    vmem = pl.BlockSpec(memory_space=pltpu.VMEM)
    out = jax.ShapeDtypeStruct((rows, features), BF16)
    tiles = pltpu.VMEM((NBLK, CHUNK, D_HEAD), BF16)
    picked = pltpu.VMEM((len(SERVED), ENTRIES, CHUNK, D_HEAD), BF16)
    far = pltpu.VMEM((ENTRIES, heads, BLK, D_HEAD), BF16)
    got = pltpu.VMEM((len(SERVED), ENTRIES + 1, CHUNK, D_HEAD), BF16)
    fin = pltpu.VMEM((2, heads, BLK_DEV, BLK, D_HEAD), BF16)
    near = pltpu.VMEM((heads, rows, D_HEAD), F32)
    split = (BLK_DEV, BLK, features)
    near_out = jax.ShapeDtypeStruct((heads, rows, D_HEAD), F32)
    fin_out = jax.ShapeDtypeStruct((2, heads, BLK_DEV, BLK, D_HEAD), BF16)
    outs = pl.pallas_call(
        functools.partial(kernel, tp_size),
        out_shape=(out, out, near_out, fin_out),
        in_specs=[smem, smem, vmem] + [anywhere] * 5,
        out_specs=(anywhere,) * 4,
        scratch_shapes=[
            pltpu.VMEM(grad_out.shape, BF16),
            pltpu.VMEM(out_weight.shape, BF16),
            pltpu.VMEM(queries.shape, BF16),
            pltpu.VMEM(split, BF16),
            pltpu.VMEM(split, BF16),
            pltpu.VMEM((tp_size,) + grad_out.shape, BF16),
            pltpu.VMEM(queries.shape, BF16),
            tiles, tiles, picked, picked, far, far,
            far, far, got, got, tiles, tiles, fin,
            pltpu.VMEM(queries.shape, BF16),
            pltpu.VMEM(queries.shape, BF16),
            pltpu.VMEM((heads, rows, rows), F32),
            pltpu.VMEM((heads, BLK_DEV, NREM * BLK, BLK), F32),
            near, near,
            pltpu.VMEM((NBLK, NBLK), jnp.int32),
            pltpu.SMEM((NBLK, NBLK), jnp.int32),
            pltpu.SemaphoreType.DMA((9,)),
            pltpu.SemaphoreType.DMA((9,)),
            pltpu.SemaphoreType.DMA((6,)),
            pltpu.SemaphoreType.DMA((3,)),
            pltpu.SemaphoreType.REGULAR,
            pltpu.SemaphoreType.REGULAR,
        ],
        compiler_params=pltpu.CompilerParams(
            collective_id=0, has_side_effects=True, vmem_limit_bytes=56 * 2**20
        ),
    )(
        listed, live, listed,
        grad_out, out_weight, queries, keys.reshape(split), values.reshape(split),
    )
    return pl.pallas_call(
        write_out,
        out_shape=(out, out, out),
        in_specs=[anywhere] * 4,
        out_specs=(anywhere,) * 3,
        scratch_shapes=[
            pltpu.VMEM(queries.shape, BF16),
            pltpu.VMEM(queries.shape, BF16),
            near, fin,
            pltpu.VMEM(queries.shape, BF16),
            pltpu.SemaphoreType.DMA((2 * heads + 2,)),
            pltpu.SemaphoreType.DMA((heads + 2,)),
        ],
    )(*outs)


def solution(mesh):
    placed = (
        P("seq", "tp"),
        P("tp", None),
        P("seq", "tp"),
        P("seq", "tp"),
        P("seq", "tp"),
        P(),
        P(),
    )
    return jax.shard_map(
        functools.partial(shards, mesh.shape["tp"]),
        mesh=mesh,
        in_specs=placed,
        out_specs=(P("seq", "tp"), P("seq", "tp"), P("seq", "tp")),
        check_vma=False,
    )
```

```python
import functools
import math

import jax
import jax.numpy as jnp
from jax import lax
from jax.experimental import pallas as pl
from jax.experimental.pallas import tpu as pltpu
from jax.sharding import PartitionSpec as P

MESH = pl.DeviceIdType.MESH
BF16 = jnp.bfloat16
F32 = jnp.float32

D_HEAD = 128
BLK = 128
BLK_DEV = 2
NREM = 3
ENTRIES = BLK_DEV * NREM
NZ, NX = 8, 4
SHARDS = NZ * NX
NBLK = SHARDS * BLK_DEV
CHUNK = 32
HALF = CHUNK // 2
SCALE = 1.0 / math.sqrt(D_HEAD)

SERVED = (
    [(dz, dx, 0, CHUNK) for dz in (0, 1, NZ - 1) for dx in range(NX)]
    + [(2, dx, HALF, HALF) for dx in range(NX)]
    + [(NZ - 2, dx, 0, HALF) for dx in range(NX)]
)
SLOT = {(dz, dx): i for i, (dz, dx, _, _) in enumerate(SERVED)}
FULL_SLOTS = 16

P1K, P1V, P2K, P2V, R1V, R1K, R2V, R2K, GATHER = range(9)


def dot(a, b, contract):
    return lax.dot_general(a, b, ((contract[:1], contract[1:]), ((), ())), preferred_element_type=F32)


def add_terms(near, fin, out, head):
    total = near[head]
    for copy in range(2):
        total += fin[copy, head].reshape(BLK_DEV * BLK, D_HEAD).astype(F32)
    out[:, head * D_HEAD : (head + 1) * D_HEAD] = total.astype(BF16)


def kernel(
    tp_size,
    visible, live, listed,
    g_hbm, w_hbm, q_hbm, k_hbm, v_hbm,
    dq_hbm, dv_hbm, near_dk_hbm, fin_k,
    g_v, w_v, q_v, k_v, v_v, g_all, do_v,
    hold_k, hold_v, pick_k, pick_v, far_k, far_v,
    back_v, back_k, got_v, got_k, sum_v, sum_k, fin_v,
    dq_ref, dv_ref, near_p, far_p, near_dv, near_dk, found, inverse,
    send, recv, load, store, upward, downward,
):
    me = lax.axis_index("seq")
    tp = lax.axis_index("tp")
    z, x = lax.div(me, NX), lax.rem(me, NX)
    others = [(dz, dx) for dz in range(NZ) for dx in range(NX) if (dz, dx) != (0, 0)]

    def shard_at(dz, dx):
        return lax.rem(z + dz, NZ) * NX + lax.rem(x + dx, NX)

    barrier = pltpu.get_barrier_semaphore()
    greeted = [(1, 0), (NZ - 1, 0)] + [(0, dx) for dx in range(1, NX)]
    for dz, dx in greeted:
        pl.semaphore_signal(barrier, inc=1, device_id=(shard_at(dz, dx), tp), device_id_type=MESH)
    for dt in range(1, tp_size):
        pl.semaphore_signal(barrier, inc=1, device_id=(me, lax.rem(tp + dt, tp_size)), device_id_type=MESH)
    loads = [
        pltpu.make_async_copy(src, dst, load.at[i])
        for i, (src, dst) in enumerate(((k_hbm, k_v), (g_hbm, g_v), (v_hbm, v_v), (q_hbm, q_v), (w_hbm, w_v)))
    ]
    for copy in loads:
        copy.start()
    shape = (NBLK, NBLK)
    block = lax.broadcasted_iota(jnp.int32, shape, 0)
    first_entry = lax.broadcasted_iota(jnp.int32, shape, 1) % BLK_DEV * NREM
    place = jnp.full(shape, ENTRIES, jnp.int32)
    for j in range(NREM):
        place = jnp.where(listed[j : j + 1, :] == block, first_entry + j, place)
    found[...] = place
    table = pltpu.make_async_copy(found, inverse, load.at[5])
    table.start()
    loads[0].wait()
    loads[1].wait()
    loads[2].wait()
    pl.semaphore_wait(barrier, len(greeted) + tp_size - 1)

    def remote(src, dst, phase, device):
        pltpu.make_async_remote_copy(
            src_ref=src, dst_ref=dst, send_sem=send.at[phase], recv_sem=recv.at[phase],
            device_id=device, device_id_type=MESH,
        ).start()

    def local(src, dst, phase):
        pltpu.make_async_copy(src, dst, recv.at[phase]).start()

    def arrived(ref, phase):
        pltpu.make_async_copy(ref, ref, recv.at[phase]).wait()

    def sent(ref, phase):
        pltpu.make_async_copy(ref, ref, send.at[phase]).wait()

    def chunk_of(zz):
        return pl.multiple_of(lax.rem(zz, NX) * CHUNK, CHUNK)

    def lanes_of(head):
        return pl.ds(pl.multiple_of(head * D_HEAD, D_HEAD), D_HEAD)

    my_blocks = pl.ds(me * BLK_DEV, BLK_DEV)

    def spread(own, hold, phase, dz):
        for dx in range(NX):
            src = own.at[:, pl.ds(chunk_of(z + dz), CHUNK), lanes_of(lax.rem(x + dx, NX))]
            if (dz, dx) == (0, 0):
                local(src, hold.at[my_blocks], phase)
            else:
                remote(src, hold.at[my_blocks], phase, (shard_at(dz, dx), tp))

    def tell(semaphore, dz):
        pl.semaphore_signal(semaphore, inc=1, device_id=(shard_at(dz, 0), tp), device_id_type=MESH)

    tell(upward, NZ - 1)
    tell(downward, 1)
    spread(k_v, hold_k, P1K, 0)
    half = NZ // 2
    for step in range(1, half + 1):
        pl.semaphore_wait(upward, 1)
        if step < half:
            tell(upward, NZ - 1)
        spread(k_v, hold_k, P1K, step)
        if step < half:
            pl.semaphore_wait(downward, 1)
            if step < half - 1:
                tell(downward, 1)
            spread(k_v, hold_k, P1K, NZ - step)
            if step == 2:
                spread(v_v, hold_v, P1V, 0)
            if step >= 2:
                spread(v_v, hold_v, P1V, step - 1)
                spread(v_v, hold_v, P1V, NZ - step + 1)
    for dt in range(1, tp_size):
        remote(g_v, g_all.at[tp], GATHER, (me, lax.rem(tp + dt, tp_size)))
    local(g_v, g_all.at[tp], GATHER)
    for dz in range(half - 1, half + 2):
        spread(v_v, hold_v, P1V, dz)

    loads[3].wait()

    def near_scores(head, _):
        lanes = lanes_of(head)
        keys = k_v[:, :, lanes].reshape(BLK_DEV * BLK, D_HEAD)
        near_p[head] = dot(keys, q_v[:, lanes], (1, 1)) * SCALE
        return 0

    lax.fori_loop(0, NX, near_scores, 0)

    def forward(hold, pick, far, phase):
        for i, (dz, dx, first, rows) in enumerate(SERVED):
            shard = shard_at(dz, dx)
            for e in range(ENTRIES):
                block = visible[e % NREM, shard * BLK_DEV + e // NREM]
                pick[i, e, first : first + rows] = hold[block, first : first + rows]
        for i, (dz, dx, first, rows) in enumerate(SERVED):
            src = pick.at[i, :, pl.ds(first, rows)]
            dst = far.at[:, x, pl.ds(pl.multiple_of(chunk_of(z) + first, HALF), rows)]
            if i == 0:
                local(src, dst, phase)
            else:
                remote(src, dst, phase, (shard_at(dz, dx), tp))

    arrived(hold_k, P1K)
    forward(hold_k, pick_k, far_k, P2K)
    arrived(hold_v, P1V)
    forward(hold_v, pick_v, far_v, P2V)

    loads[4].wait()
    arrived(g_all, GATHER)
    width = g_v.shape[1]
    total = dot(g_all[0], w_v[:, :width], (1, 1))
    for t in range(1, tp_size):
        total += dot(g_all[t], w_v[:, t * width : (t + 1) * width], (1, 1))
    do_v[...] = total.astype(BF16)

    def return_far(back, got, phase, dx):
        head = lax.rem(x + dx, NX)
        for dz in (0, 1, NZ - 1, 2, NZ - 2):
            slot = SLOT[((NZ - dz) % NZ, (NX - dx) % NX)]
            _, _, first, rows = SERVED[slot]
            src = back.at[:, head, pl.ds(pl.multiple_of(chunk_of(z + dz) + first, HALF), rows)]
            dst = got.at[slot, pl.ds(0, ENTRIES), pl.ds(first, rows)]
            if slot == 0:
                local(src, dst, phase)
            else:
                remote(src, dst, phase, (shard_at(dz, dx), tp))

    arrived(far_k, P2K)
    for dx in range(NX):
        head = lax.rem(x + dx, NX)
        lanes = lanes_of(head)
        pieces = []
        for a in range(BLK_DEV):
            rows = slice(a * BLK, (a + 1) * BLK)
            near = near_p[head, :, rows]
            keys = far_k[a * NREM : (a + 1) * NREM, head].reshape(NREM * BLK, D_HEAD)
            far = dot(keys, q_v[rows, lanes], (1, 1)) * SCALE
            count = live[me * BLK_DEV + a]
            entry = lax.broadcasted_iota(jnp.int32, far.shape, 0) // BLK
            far = jnp.where(entry < count, far, -1e30)
            highest = jnp.maximum(jnp.max(near, axis=0, keepdims=True), jnp.max(far, axis=0, keepdims=True))
            near = jnp.exp(near - highest)
            far = jnp.exp(far - highest)
            scale = 1.0 / (jnp.sum(near, axis=0, keepdims=True) + jnp.sum(far, axis=0, keepdims=True))
            near = near * scale
            far = far * scale
            near_p[head, :, rows] = near
            far_p[head, a] = far
            far_dv = dot(far.astype(BF16), do_v[rows, lanes], (1, 0)).astype(BF16)
            back_v[a * NREM : (a + 1) * NREM, head] = far_dv.reshape(NREM, BLK, D_HEAD)
            pieces.append(near.astype(BF16))
        return_far(back_v, got_v, R1V, dx)
        near_dv[head] = dot(jnp.concatenate(pieces, axis=1), do_v[:, lanes], (1, 0))

    arrived(far_v, P2V)
    for dx in range(NX):
        head = lax.rem(x + dx, NX)
        lanes = lanes_of(head)
        values = v_v[:, :, lanes].reshape(BLK_DEV * BLK, D_HEAD)
        near_grad = dot(values, do_v[:, lanes], (1, 1))
        pieces, fars = [], []
        for a in range(BLK_DEV):
            rows = slice(a * BLK, (a + 1) * BLK)
            far_values = far_v[a * NREM : (a + 1) * NREM, head].reshape(NREM * BLK, D_HEAD)
            grad = dot(far_values, do_v[rows, lanes], (1, 1))
            near, far = near_p[head, :, rows], far_p[head, a]
            own = near_grad[:, rows]
            delta = jnp.sum(near * own, axis=0, keepdims=True) + jnp.sum(far * grad, axis=0, keepdims=True)
            near = (near * (own - delta) * SCALE).astype(BF16)
            far = (far * (grad - delta) * SCALE).astype(BF16)
            far_dk = dot(far, q_v[rows, lanes], (1, 0)).astype(BF16)
            back_k[a * NREM : (a + 1) * NREM, head] = far_dk.reshape(NREM, BLK, D_HEAD)
            pieces.append(near)
            fars.append(far)
        return_far(back_k, got_k, R1K, dx)
        near = jnp.concatenate(pieces, axis=1)
        near_dk[head] = dot(near, q_v[:, lanes], (1, 0))
        keys = k_v[:, :, lanes].reshape(BLK_DEV * BLK, D_HEAD)
        near_dq = dot(near, keys, (0, 0))
        for a in range(BLK_DEV):
            rows = slice(a * BLK, (a + 1) * BLK)
            keys = far_k[a * NREM : (a + 1) * NREM, head].reshape(NREM * BLK, D_HEAD)
            dq_ref[rows, lanes] = (near_dq[rows] + dot(fars[a], keys, (0, 0))).astype(BF16)

    stores = [
        pltpu.make_async_copy(src, dst, store.at[i])
        for i, (src, dst) in enumerate(((dq_ref, dq_hbm), (near_dk, near_dk_hbm), (dv_ref, dv_hbm)))
    ]
    stores[0].start()
    stores[1].start()

    served = [shard_at(dz, dx) * BLK_DEV for dz, dx, _, _ in SERVED]
    table.wait()
    zeros = jnp.zeros((CHUNK, D_HEAD), BF16)

    def collect(got, sums, fin, phase):
        def one_block(block, _):
            upper = jnp.zeros((HALF, D_HEAD), F32)
            lower = jnp.zeros((HALF, D_HEAD), F32)
            for i, (_, _, first, rows) in enumerate(SERVED):
                e = jnp.minimum(inverse[block, served[i]], inverse[block, served[i] + 1])
                if first == 0:
                    upper += got[i, e, :HALF].astype(F32)
                if first + rows == CHUNK:
                    lower += got[i, e, HALF:].astype(F32)
            sums[block, :HALF] = upper.astype(BF16)
            sums[block, HALF:] = lower.astype(BF16)
            return 0

        lax.fori_loop(0, NBLK, one_block, 0)
        dst = fin.at[lax.div(z, NX), x, :, pl.ds(chunk_of(z), CHUNK)]
        for dz, dx in others:
            shard = shard_at(dz, dx)
            remote(sums.at[pl.ds(shard * BLK_DEV, BLK_DEV)], dst, phase, (shard, tp))
        local(sums.at[my_blocks], dst, phase)

    counted = (pl.ds(0, FULL_SLOTS), pl.ds(0, ENTRIES))
    for i in range(len(SERVED)):
        got_v[i, ENTRIES] = zeros
        got_k[i, ENTRIES] = zeros
    arrived(got_v.at[counted], R1V)
    collect(got_v, sum_v, fin_v, R2V)
    arrived(got_k.at[counted], R1K)
    collect(got_k, sum_k, fin_k, R2K)

    arrived(fin_v, R2V)
    for head in range(NX):
        add_terms(near_dv, fin_v, dv_ref, head)
    stores[2].start()
    for copy in stores:
        copy.wait()

    most = pl.ds(0, NBLK - BLK_DEV)
    sent(hold_k.at[most], P1K)
    sent(hold_v.at[most], P1V)
    sent(g_all.at[pl.ds(0, tp_size - 1)], GATHER)
    fewer = (pl.ds(0, FULL_SLOTS - 1), pl.ds(0, ENTRIES))
    sent(pick_k.at[fewer], P2K)
    sent(pick_v.at[fewer], P2V)
    sent(got_v.at[fewer], R1V)
    sent(got_k.at[fewer], R1K)
    sent(sum_v.at[most], R2V)
    sent(sum_k.at[most], R2K)
    arrived(fin_k, R2K)


def write_out(dq, dv, near_dk, fin_k, dq_out, dk_out, dv_out, dq_v, dv_v, near_v, fin_v, dk_v, taken, put):
    heads = near_dk.shape[0]
    takes, puts = [], []
    for head in range(heads):
        lanes = pl.ds(head * D_HEAD, D_HEAD)
        takes.append((
            pltpu.make_async_copy(fin_k.at[:, head], fin_v.at[:, head], taken.at[2 * head]),
            pltpu.make_async_copy(near_dk.at[head], near_v.at[head], taken.at[2 * head + 1]),
        ))
        puts.append(pltpu.make_async_copy(dk_v.at[:, lanes], dk_out.at[:, lanes], put.at[head]))
    whole = ((dq, dq_v, dq_out), (dv, dv_v, dv_out))
    for i, (src, held, dst) in enumerate(whole):
        takes.append((pltpu.make_async_copy(src, held, taken.at[2 * heads + i]),))
        puts.append(pltpu.make_async_copy(held, dst, put.at[heads + i]))
    order = [heads, heads + 1] + list(range(heads))
    for i in order:
        for copy in takes[i]:
            copy.start()
    for i in order:
        for copy in takes[i]:
            copy.wait()
        if i < heads:
            add_terms(near_v, fin_v, dk_v, i)
        puts[i].start()
    for copy in puts:
        copy.wait()


def shards(tp_size, grad_out, out_weight, queries, keys, values, visible, live):
    rows, features = queries.shape
    heads = features // D_HEAD
    listed = visible.astype(jnp.int32).T
    smem = pl.BlockSpec(memory_space=pltpu.SMEM)
    anywhere = pl.BlockSpec(memory_space=pltpu.HBM)
    vmem = pl.BlockSpec(memory_space=pltpu.VMEM)
    out = jax.ShapeDtypeStruct((rows, features), BF16)
    tiles = pltpu.VMEM((NBLK, CHUNK, D_HEAD), BF16)
    picked = pltpu.VMEM((len(SERVED), ENTRIES, CHUNK, D_HEAD), BF16)
    far = pltpu.VMEM((ENTRIES, heads, BLK, D_HEAD), BF16)
    got = pltpu.VMEM((len(SERVED), ENTRIES + 1, CHUNK, D_HEAD), BF16)
    fin = pltpu.VMEM((2, heads, BLK_DEV, BLK, D_HEAD), BF16)
    near = pltpu.VMEM((heads, rows, D_HEAD), F32)
    split = (BLK_DEV, BLK, features)
    near_out = jax.ShapeDtypeStruct((heads, rows, D_HEAD), F32)
    fin_out = jax.ShapeDtypeStruct((2, heads, BLK_DEV, BLK, D_HEAD), BF16)
    outs = pl.pallas_call(
        functools.partial(kernel, tp_size),
        out_shape=(out, out, near_out, fin_out),
        in_specs=[smem, smem, vmem] + [anywhere] * 5,
        out_specs=(anywhere,) * 4,
        scratch_shapes=[
            pltpu.VMEM(grad_out.shape, BF16),
            pltpu.VMEM(out_weight.shape, BF16),
            pltpu.VMEM(queries.shape, BF16),
            pltpu.VMEM(split, BF16),
            pltpu.VMEM(split, BF16),
            pltpu.VMEM((tp_size,) + grad_out.shape, BF16),
            pltpu.VMEM(queries.shape, BF16),
            tiles, tiles, picked, picked, far, far,
            far, far, got, got, tiles, tiles, fin,
            pltpu.VMEM(queries.shape, BF16),
            pltpu.VMEM(queries.shape, BF16),
            pltpu.VMEM((heads, rows, rows), F32),
            pltpu.VMEM((heads, BLK_DEV, NREM * BLK, BLK), F32),
            near, near,
            pltpu.VMEM((NBLK, NBLK), jnp.int32),
            pltpu.SMEM((NBLK, NBLK), jnp.int32),
            pltpu.SemaphoreType.DMA((9,)),
            pltpu.SemaphoreType.DMA((9,)),
            pltpu.SemaphoreType.DMA((6,)),
            pltpu.SemaphoreType.DMA((3,)),
            pltpu.SemaphoreType.REGULAR,
            pltpu.SemaphoreType.REGULAR,
        ],
        compiler_params=pltpu.CompilerParams(
            collective_id=0, has_side_effects=True, vmem_limit_bytes=56 * 2**20
        ),
    )(
        listed, live, listed,
        grad_out, out_weight, queries, keys.reshape(split), values.reshape(split),
    )
    return pl.pallas_call(
        write_out,
        out_shape=(out, out, out),
        in_specs=[anywhere] * 4,
        out_specs=(anywhere,) * 3,
        scratch_shapes=[
            pltpu.VMEM(queries.shape, BF16),
            pltpu.VMEM(queries.shape, BF16),
            near, fin,
            pltpu.VMEM(queries.shape, BF16),
            pltpu.SemaphoreType.DMA((2 * heads + 2,)),
            pltpu.SemaphoreType.DMA((heads + 2,)),
        ],
    )(*outs)


def solution(mesh):
    placed = (
        P("seq", "tp"),
        P("tp", None),
        P("seq", "tp"),
        P("seq", "tp"),
        P("seq", "tp"),
        P(),
        P(),
    )
    return jax.shard_map(
        functools.partial(shards, mesh.shape["tp"]),
        mesh=mesh,
        in_specs=placed,
        out_specs=(P("seq", "tp"), P("seq", "tp"), P("seq", "tp")),
        check_vma=False,
    )
```
